256 devices in a mesh: group: 8 (over x, core), inner: 32 (over z, y).
Axes of the slice: x: 4, y: 4, z: 8, core: 2. Of those that a mesh axis runs over, the one named last changes fastest.
Arguments:
- x_self: bfloat16 [262144, 256], P(('group', 'inner')), may hold values from -6 to 6
- x_agg: bfloat16 [262144, 256], P(('group', 'inner')), may hold values from -6 to 6
- w_self: bfloat16 [256, 256], replicated, may hold values from -0.25 to 0.25
- w_nbr: bfloat16 [256, 256], replicated, may hold values from -0.25 to 0.25
- b_layer: float32 [256], replicated, may hold values from -3 to 3
- w_one: bfloat16 [256, 512], replicated, may hold values from -0.375 to 0.375
- b_one: float32 [512], replicated, may hold values from -3 to 3
- w_two: bfloat16 [512, 512], replicated, may hold values from -0.25 to 0.25
- b_two: float32 [512], replicated, may hold values from -3 to 3
- w_out: float32 [512], replicated, may hold values from -2 to 2
- send_lists: int32 [2048, 32, 12], P(('group', 'inner')), may hold values from 0 to 1023, as said below
- endpoint_slots: int32 [131072, 2], P(('group', 'inner')), may hold values from 0 to 3071, as said below
- neg_index: int32 [131072, 4], P(('group', 'inner')), may hold values from 0 to 511, as said below
Outputs:
- grad_self: bfloat16 [262144, 256], P(('group', 'inner'))
- grad_agg: bfloat16 [262144, 256], P(('group', 'inner'))
- grad_scorer: float32 [393216], P(('group', 'inner'))
- grad_layer: float32 [131072], P(('group', 'inner'))
- grad_bias: float32 [1792], replicated
The draws below stay inside these ranges and needn't reach their ends.
Inputs may be any that keep to these rules, and one draw needn't show every extreme that they name: `send_lists`: viewed as [256, 256, 12] (owner, requesting device, slot), each entry is a row of the owner's block of 1024 nodes, and the 12 entries of one owner and one requesting device are distinct. Slots that endpoint_slots never names hold arbitrary rows. `endpoint_slots`: each entry of device r's block is a slot o * 12 + c of that device and names the node of send_lists' entry (o, r, c). `neg_index`: entry [p, k] is the index, within the same block of 512 positives, of another positive whose destination serves as the k-th negative of p; it is never p itself.
All inputs are finite; a program needn't handle non-finite values.
Results may differ from the reference program's by a relative error of at most 0.0075.
Values may be sent and summed in bfloat16 or wider, within the bound.
No kernel may reach another device: no remote copies, remote signals or barrier semaphores. Data moves between devices by JAX's collectives and lax.ppermute only.
A program may use at most 128 MiB of HBM per device.

```python
import jax
import jax.numpy as jnp
from jax import lax

F = 256
H = 512
POS_DEV = 512
NEG = 4
OWNERS = 256
NODE_DEV = 1024
NODES = 262144
POSITIVES = 131072
CAP = 12
PAIRS_DEV = 2560
N_GROUP = 8


def plan_counts(key):
    mean_slots = 2 * POS_DEV // OWNERS
    shuffled = jax.random.permutation(jax.random.fold_in(key, 11), OWNERS)
    owner_ids = jnp.arange(OWNERS, dtype=jnp.int32)
    hub_owner = jnp.logical_or(shuffled < max(OWNERS // 16, 1) - 1, owner_ids == OWNERS - 1)
    drawn = jax.random.randint(jax.random.fold_in(key, 12), (OWNERS, OWNERS), 1, 2 * mean_slots)
    counts = jnp.where(hub_owner[None, :], CAP, drawn).astype(jnp.int32)
    return (counts, hub_owner)


def draw_send_lists(key, part):
    counts, hub_owner = plan_counts(key)
    spread_start = jax.random.randint(jax.random.fold_in(key, 21), (OWNERS, OWNERS), 0, NODE_DEV)
    hot_start = jax.random.randint(jax.random.fold_in(key, 22), (OWNERS, OWNERS), 0, NODE_DEV // 8)
    hot_start = hot_start.at[OWNERS - 1, 0].set(NODE_DEV - CAP).at[OWNERS - 1, 1].set(0)
    stride = NODE_DEV // CAP
    slot_ids = jnp.arange(CAP, dtype=jnp.int32)
    spread_rows = (spread_start[:, :, None] + slot_ids * stride) % NODE_DEV
    packed_rows = hot_start[:, :, None] + slot_ids
    row_ids = jnp.where(hub_owner[:, None, None], packed_rows, spread_rows)
    return row_ids.reshape(OWNERS * N_GROUP, OWNERS // N_GROUP, CAP).astype(jnp.int32)


def draw_endpoint_slots(key, part):
    counts, hub_owner = plan_counts(key)
    cum_counts = jnp.cumsum(counts, axis=1)
    live_slots = cum_counts[:, -1]
    chosen = jax.random.randint(jax.random.fold_in(key, 31), (OWNERS, POS_DEV * 2), 0, live_slots[:, None])
    chosen = chosen.at[:, 0].set(live_slots - 1).at[:, 1].set(0)
    owner_ids = jax.vmap(lambda edges, picks: jnp.searchsorted(edges, picks, side='right'))(cum_counts, chosen)
    owner_ids = owner_ids.astype(jnp.int32)
    first_slot = cum_counts - counts
    offset = chosen - jnp.take_along_axis(first_slot, owner_ids, axis=1)
    slot_ids = owner_ids * CAP + offset
    return slot_ids.reshape(POSITIVES, 2).astype(jnp.int32)


def draw_neg_index(key, part):
    positions = jnp.arange(POS_DEV, dtype=jnp.int32)[None, :, None]
    shift_by = jax.random.randint(jax.random.fold_in(key, 41), (OWNERS, POS_DEV, NEG), 1, POS_DEV)
    shift_by = shift_by.at[0, 0, 0].set(POS_DEV - 1).at[0, 1, 0].set(POS_DEV - 1)
    return ((positions + shift_by) % POS_DEV).reshape(POSITIVES, NEG).astype(jnp.int32)


def block_scale(key, shape, shards, least, high):
    loudness = 1.0
    for position, shards_of in shards:
        steps = jax.random.uniform(jax.random.fold_in(jax.random.fold_in(key, 6), position), (shards_of,), jnp.float32, least / len(shards), high / len(shards))
        loudness = loudness * jnp.repeat(jnp.exp(steps), shape[position] // shards_of).reshape((-1,) + (1,) * (len(shape) - 1 - position))
    return loudness


def centred(rng, extent, spread, reach, cuts=(), held_as=jnp.bfloat16):
    gain = block_scale(rng, extent, cuts, -0.22, 0.18) if cuts else 1.0
    result = jax.random.normal(rng, extent, jnp.float32) * spread * gain
    return jnp.minimum(jnp.maximum(result, -reach), reach).astype(held_as)


def setup_inputs(seed: int = 0) -> dict:
    streams_of = jax.random.split(jax.random.key(seed), 14)
    x_self = centred(streams_of[0], (NODES, F), 1.0, 6.0, ((0, 256),))
    x_agg = centred(streams_of[1], (NODES, F), 1.0, 6.0, ((0, 256),))
    w_self = centred(streams_of[2], (F, F), (2 * F) ** -0.5, 0.25)
    w_nbr = centred(streams_of[3], (F, F), (2 * F) ** -0.5, 0.25)
    b_layer = centred(streams_of[4], (F,), 0.5, 3.0, (), jnp.float32)
    w_one = centred(streams_of[5], (F, H), F ** -0.5, 0.375)
    b_one = centred(streams_of[6], (H,), 0.5, 3.0, (), jnp.float32)
    w_two = centred(streams_of[7], (H, H), H ** -0.5, 0.25)
    b_two = centred(streams_of[8], (H,), 0.5, 3.0, (), jnp.float32)
    w_out = centred(streams_of[9], (H,), 0.3, 2.0, (), jnp.float32)
    send_lists = draw_send_lists(jax.random.fold_in(streams_of[13], 71), 0)
    endpoint_slots = draw_endpoint_slots(jax.random.fold_in(streams_of[13], 71), 0)
    neg_index = draw_neg_index(jax.random.fold_in(streams_of[13], 71), 0)
    return dict(x_self=x_self, x_agg=x_agg, w_self=w_self, w_nbr=w_nbr, b_layer=b_layer, w_one=w_one, b_one=b_one, w_two=w_two, b_two=b_two, w_out=w_out, send_lists=send_lists, endpoint_slots=endpoint_slots, neg_index=neg_index)


def silu_slope(inputs):
    sigmoid_of = jax.nn.sigmoid(inputs)
    return sigmoid_of * (1.0 + inputs * (1.0 - sigmoid_of))


def dot_first(first_op, second_op):
    return lax.dot_general(first_op, second_op, (((0,), (0,)), ((), ())), preferred_element_type=jnp.float32)


def dot_last(first_op, second_op):
    return lax.dot_general(first_op, second_op, (((1,), (1,)), ((), ())), preferred_element_type=jnp.float32)


def reference(x_self, x_agg, w_self, w_nbr, b_layer, w_one, b_one, w_two, b_two, w_out, send_lists, endpoint_slots, neg_index):
    pre_act = jnp.dot(x_self, w_self, preferred_element_type=jnp.float32) + jnp.dot(x_agg, w_nbr, preferred_element_type=jnp.float32) + b_layer
    node_table = jax.nn.silu(pre_act).astype(jnp.bfloat16)
    lists = send_lists.reshape(OWNERS, OWNERS, CAP)
    slot_blocks = endpoint_slots.reshape(OWNERS, POS_DEV, 2)
    neg_blocks = neg_index.reshape(OWNERS, POS_DEV, NEG)
    labels = (jnp.arange(PAIRS_DEV, dtype=jnp.int32) < POS_DEV).astype(jnp.float32)

    def requester_step(carry, inputs):
        node_grads, grad_first, grad_second, bias_one, bias_two, bias_out = carry
        requester, slot_block, neg_block = inputs
        owner_ids = slot_block // CAP
        column = slot_block % CAP
        owner_rows = lists[owner_ids, requester, column]
        node_ids = (owner_ids * NODE_DEV + owner_rows).astype(jnp.int32)
        neg_flat = neg_block.T.reshape(-1)
        src_nodes = node_ids[:, 0]
        dst_nodes = node_ids[:, 1]
        left_nodes = jnp.tile(src_nodes, 1 + NEG)
        right_nodes = jnp.concatenate([dst_nodes, dst_nodes[neg_flat]])
        left_rows = node_table[left_nodes]
        right_rows = node_table[right_nodes]
        joint_rows = (left_rows.astype(jnp.float32) * right_rows.astype(jnp.float32)).astype(jnp.bfloat16)
        a_one = jnp.dot(joint_rows, w_one, preferred_element_type=jnp.float32) + b_one
        h_one = jax.nn.silu(a_one).astype(jnp.bfloat16)
        a_two = jnp.dot(h_one, w_two, preferred_element_type=jnp.float32) + b_two
        h_two = jax.nn.silu(a_two)
        scores = jnp.sum(h_two * w_out, axis=1)
        loss_slope = jax.nn.sigmoid(scores) - labels
        d_two = (loss_slope[:, None] * w_out) * silu_slope(a_two)
        d_two_low = d_two.astype(jnp.bfloat16)
        d_one = dot_last(d_two_low, w_two) * silu_slope(a_one)
        d_one_low = d_one.astype(jnp.bfloat16)
        d_joint = dot_last(d_one_low, w_one)
        d_left = d_joint * right_rows.astype(jnp.float32)
        d_right = d_joint * left_rows.astype(jnp.float32)
        node_grads = node_grads.at[left_nodes].add(d_left).at[right_nodes].add(d_right)
        grad_first = grad_first + dot_first(joint_rows, d_one_low)
        grad_second = grad_second + dot_first(h_one, d_two_low)
        bias_one = bias_one + jnp.sum(d_one, axis=0)
        bias_two = bias_two + jnp.sum(d_two, axis=0)
        bias_out = bias_out + jnp.sum(loss_slope[:, None] * h_two, axis=0)
        return (node_grads, grad_first, grad_second, bias_one, bias_two, bias_out), None

    initial = (jnp.zeros((NODES, F), jnp.float32), jnp.zeros((F, H), jnp.float32), jnp.zeros((H, H), jnp.float32),
               jnp.zeros((H,), jnp.float32), jnp.zeros((H,), jnp.float32), jnp.zeros((H,), jnp.float32))
    carried, unused = lax.scan(requester_step, initial, (jnp.arange(OWNERS, dtype=jnp.int32), slot_blocks, neg_blocks))
    node_grads, grad_first, grad_second, bias_one, bias_two, bias_out = carried
    d_pre = node_grads * silu_slope(pre_act)
    d_pre_low = d_pre.astype(jnp.bfloat16)
    grad_self = dot_last(d_pre_low, w_self).astype(jnp.bfloat16)
    grad_agg = dot_last(d_pre_low, w_nbr).astype(jnp.bfloat16)
    grad_scorer = jnp.concatenate([grad_first.reshape(-1), grad_second.reshape(-1)]) / PAIRS_DEV
    grad_layer = jnp.concatenate([dot_first(x_self, d_pre_low).reshape(-1), dot_first(x_agg, d_pre_low).reshape(-1)]) / PAIRS_DEV
    grad_bias = jnp.concatenate([bias_one, bias_two, bias_out, jnp.sum(d_pre, axis=0)]) / PAIRS_DEV
    return (grad_self, grad_agg, grad_scorer, grad_layer, grad_bias)
```

```python
import jax
import jax.numpy as jnp
from jax import lax
from jax.experimental import pallas as pl
from jax.experimental.pallas import tpu as pltpu
from jax.sharding import PartitionSpec as P

F32 = jnp.float32
BF16 = jnp.bfloat16


def dot(a, b):
    return jnp.dot(a, b, preferred_element_type=F32)


def dot_first(a, b):
    return lax.dot_general(a, b, (((0,), (0,)), ((), ())), preferred_element_type=F32)


def dot_last(a, b):
    return lax.dot_general(a, b, (((1,), (1,)), ((), ())), preferred_element_type=F32)


def sigm(v):
    return 0.5 + 0.5 * jnp.tanh(0.5 * v)


def one_hot(a, b):
    return jnp.where(a == b, 1.0, 0.0).astype(BF16)


def layer_kernel(xs, xa, ws, wn, bl, idx, send, slope, tab):
    nodes = xs.shape[0]
    for r in range(nodes // 256):
        rows = pl.ds(r * 256, 256)
        pre = dot(xs[rows, :], ws[...]) + dot(xa[rows, :], wn[...]) + bl[...]
        s = sigm(pre)
        t = pre * s
        tab[rows, :] = t.astype(BF16)
        slope[rows, :] = s + t * (1.0 - s)
    owners = send.shape[0]
    node_ids = lax.broadcasted_iota(jnp.int32, (256, nodes), 1)

    def full(b, carry):
        y = dot(one_hot(idx[pl.ds(b * 256, 256), :], node_ids), tab[...]).astype(BF16)
        send[pl.ds(b * 32, 32), 0:8, :] = y[:, :128].reshape(32, 8, 128)
        send[pl.ds(b * 32, 32), 8:16, :] = y[:, 128:].reshape(32, 8, 128)
        return carry

    lax.fori_loop(0, owners // 32, full, 0)
    low = lax.broadcasted_iota(jnp.int32, (256, 128), 0) % 8 < 4

    def mixed(b, carry):
        y = dot(one_hot(idx[pl.ds(owners * 8 + b * 256, 256), :], node_ids), tab[...])
        y = jnp.where(low, y[:, :128], y[:, 128:]).astype(BF16)
        send[pl.ds(b * 32, 32), 16:24, :] = y.reshape(32, 8, 128)
        return carry

    lax.fori_loop(0, owners // 32, mixed, 0)


def unpack(chunks, rows_ref):
    half = chunks.shape[0] * 8
    rows_ref[0:half, 0:128] = chunks[:, 0:8, :].reshape(half, 128)
    rows_ref[0:half, 128:256] = chunks[:, 8:16, :].reshape(half, 128)
    tail = chunks[:, 16:24, :].reshape(half, 128).astype(F32)
    rows_ref[half:, 0:128] = tail.astype(BF16)
    rows_ref[half:, 128:256] = pltpu.roll(tail, half - 4, 0).astype(BF16)


def scorer_kernel(
    chunks, pcol, plane, ncol, nlane, w1, b1, w2, b2, wo,
    out, scorer, bias,
    rows, ends, grads, split, joint, right, h1, sl1, a1, a2, d2, gw1, gw2,
):
    owners = chunks.shape[0]
    table = owners * 16
    pos = ends.shape[0] // 2
    unpack(chunks, rows)
    slot_ids = lax.broadcasted_iota(jnp.int32, (256, table), 1)

    def fetch(b, carry):
        at = pl.ds(b * 256, 256)
        ends[at, :] = dot(one_hot(pcol[at, :], slot_ids), rows[...]).astype(BF16)
        return carry

    lax.fori_loop(0, 2 * pos // 256, fetch, 0)
    src = ends.at[0:pos, :]
    dst = ends.at[pos : 2 * pos, :]
    grads[...] = jnp.zeros_like(grads)
    gw1[...] = jnp.zeros_like(gw1)
    gw2[...] = jnp.zeros_like(gw2)
    bias[...] = jnp.zeros_like(bias)
    step = 64

    def block(label):
        joint[...] = (src[...].astype(F32) * right[...].astype(F32)).astype(BF16)
        a1[...] = dot(joint[...], w1[...]) + b1[...]

        def first(c, carry):
            at = pl.ds(c * step, step)
            v = a1[at, :]
            s = sigm(v)
            h = v * s
            h1[at, :] = h.astype(BF16)
            sl1[at, :] = s + h * (1.0 - s)
            return carry

        lax.fori_loop(0, pos // step, first, 0)
        a2[...] = dot(h1[...], w2[...]) + b2[...]

        def second(c, carry):
            sum2, sumo = carry
            at = pl.ds(c * step, step)
            v = a2[at, :]
            s = sigm(v)
            h = v * s
            score = jnp.sum(h * wo[...], axis=1, keepdims=True)
            ls = sigm(score) - label
            d = ls * wo[...] * (s + h * (1.0 - s))
            d2[at, :] = d.astype(BF16)
            return (
                sum2 + jnp.sum(d.reshape(step // 8, 8, -1), axis=0),
                sumo + jnp.sum((ls * h).reshape(step // 8, 8, -1), axis=0),
            )

        zero = jnp.zeros((8, w2.shape[1]), F32)
        sum2, sumo = lax.fori_loop(0, pos // step, second, (zero, zero))
        bias[8:16, :] += sum2
        bias[16:24, :] += sumo
        a1[...] = dot_last(d2[...], w2[...])

        def third(c, carry):
            at = pl.ds(c * step, step)
            d = a1[at, :] * sl1[at, :]
            a1[at, :] = d
            return carry + jnp.sum(d.reshape(step // 8, 8, -1), axis=0)

        bias[0:8, :] += lax.fori_loop(0, pos // step, third, zero)
        d1 = a1[...].astype(BF16)
        gw1[...] += dot_first(joint[...], d1)
        gw2[...] += dot_first(h1[...], d2[...])
        dj = dot_last(d1, w1[...])
        grads[0:pos, :] += dj * right[...].astype(F32)
        return dj * src[...].astype(F32)

    right[...] = dst[...]
    grads[pos:, :] += block(1.0)
    col_ids = lax.broadcasted_iota(jnp.int32, (pos, pos), 1)
    row_ids = lax.broadcasted_iota(jnp.int32, (pos, pos), 0)

    def negative(k, carry):
        right[...] = dot(one_hot(ncol[pl.ds(k * pos, pos), :], col_ids), dst[...]).astype(BF16)
        d_right = block(0.0)
        hi = d_right.astype(BF16)
        lo = (d_right - hi.astype(F32)).astype(BF16)
        pick = one_hot(nlane[pl.ds(k, 1), :], row_ids)
        grads[pos:, :] += dot(pick, hi) + dot(pick, lo)
        return carry

    lax.fori_loop(0, nlane.shape[0], negative, 0)
    hi = grads[...].astype(BF16)
    split[:, 0:256] = hi
    split[:, 256:512] = (grads[...] - hi.astype(F32)).astype(BF16)
    sub = lax.broadcasted_iota(jnp.int32, (256, 2 * pos), 0)
    sub_mixed = sub - (sub & 4)

    def spread(ids):
        y = dot(one_hot(plane[...], ids), split[...])
        return y[:, 0:256] + y[:, 256:512]

    def full(b, carry):
        y = spread(sub + b * 256).astype(BF16)
        out[pl.ds(b * 32, 32), 0:8, :] = y[:, :128].reshape(32, 8, 128)
        out[pl.ds(b * 32, 32), 8:16, :] = y[:, 128:].reshape(32, 8, 128)
        return carry

    lax.fori_loop(0, owners // 32, full, 0)
    low = lax.broadcasted_iota(jnp.int32, (256, 128), 0) % 8 < 4

    def mixed(b, carry):
        y = spread(sub_mixed + (owners * 8 + b * 256))
        y = jnp.where(low, y[:, :128], y[:, 128:]).astype(BF16)
        out[pl.ds(b * 32, 32), 16:24, :] = y.reshape(32, 8, 128)
        return carry

    lax.fori_loop(0, owners // 32, mixed, 0)
    for g in range(8):
        for q in range(4):
            cols = slice(q * 128, q * 128 + 128)
            lo_row = g * 96
            at = q * 96
            n1 = min(max(256 - lo_row, 0), 96)
            if n1 > 0:
                scorer[g, at : at + n1, :] = gw1[lo_row : lo_row + n1, cols].astype(BF16)
            if n1 < 96:
                first_row = lo_row + n1 - 256
                scorer[g, at + n1 : at + 96, :] = gw2[first_row : first_row + 96 - n1, cols].astype(BF16)


def owner_kernel(
    chunks, lanes, slope, xs, xa, ws, wn, scorer, bias,
    gself, gagg, terms,
    rows, dpre, sums,
):
    table = lanes.shape[1]
    nodes = xs.shape[0]
    unpack(chunks, rows)
    ids = lax.broadcasted_iota(jnp.int32, (256, table), 0)

    def nodes_step(b, carry):
        at = pl.ds(b * 256, 256)
        d = dot(one_hot(lanes[...], ids + b * 256), rows[...]) * slope[at, :]
        low = d.astype(BF16)
        dpre[at, :] = low
        gself[at, :] = dot_last(low, ws[...]).astype(BF16)
        gagg[at, :] = dot_last(low, wn[...]).astype(BF16)
        return carry + jnp.sum(d.reshape(32, 8, 256), axis=0)

    total = lax.fori_loop(0, nodes // 256, nodes_step, jnp.zeros((8, 256), F32))
    total = jnp.sum(total, axis=0, keepdims=True)
    sums[...] = jnp.zeros_like(sums)
    for part in range(3):
        whole = jnp.sum(bias[part * 8 : part * 8 + 8, :], axis=0, keepdims=True)
        for q in range(4):
            sums[part * 4 + q : part * 4 + q + 1, :] = whole[:, q * 128 : q * 128 + 128]
    for q in range(2):
        sums[12 + q : 13 + q, :] = total[:, q * 128 : q * 128 + 128]
    hi = sums[0:16, :].astype(BF16)
    lo = (sums[0:16, :] - hi.astype(F32)).astype(BF16)
    parts = (dot_first(xs[...], dpre[...]), dot_first(xa[...], dpre[...]))
    for g in range(8):
        terms[g, 0:384, :] = scorer[g, :, :]
        mine = parts[g // 4]
        r = (g % 4) * 64
        for q in range(2):
            terms[g, 384 + q * 64 : 448 + q * 64, :] = mine[r : r + 64, q * 128 : q * 128 + 128].astype(BF16)
        terms[g, 512:528, :] = hi
        terms[g, 528:544, :] = lo


def body(
    x_self, x_agg, w_self, w_nbr, b_layer, w_one, b_one, w_two, b_two, w_out,
    send_lists, endpoint_slots, neg_index,
):
    nodes, width = x_self.shape
    both = ("group", "inner")
    owners = lax.axis_size("group") * lax.axis_size("inner")
    pos = endpoint_slots.shape[0]
    negs = neg_index.shape[1]
    hidden = w_one.shape[1]
    pairs = pos * (1 + negs)
    table = owners * 16
    params = pltpu.CompilerParams(vmem_limit_bytes=60 * 1024 * 1024)
    lists = send_lists.reshape(owners, 12)
    idx = jnp.concatenate(
        [lists[:, :8].reshape(-1), jnp.tile(lists[:, 8:], (1, 2)).reshape(-1)]
    ).reshape(table, 1)
    send, slope = pl.pallas_call(
        layer_kernel,
        out_shape=(
            jax.ShapeDtypeStruct((owners, 24, 128), BF16),
            jax.ShapeDtypeStruct((nodes, width), F32),
        ),
        scratch_shapes=[pltpu.VMEM((nodes, width), BF16)],
        compiler_params=params,
        name="layer",
    )(x_self, x_agg, w_self, w_nbr, b_layer.reshape(1, -1), idx)
    fetched = lax.all_to_all(send, both, 0, 0, tiled=True)
    owner = endpoint_slots // 12
    column = endpoint_slots - owner * 12
    place = jnp.where(column < 8, owner * 8 + column, owners * 8 + owner * 8 + column - 8)
    place = place.T.reshape(-1)
    neg_t = neg_index.T
    out, scorer, bias = pl.pallas_call(
        scorer_kernel,
        out_shape=(
            jax.ShapeDtypeStruct((owners, 24, 128), BF16),
            jax.ShapeDtypeStruct((8, 384, 128), BF16),
            jax.ShapeDtypeStruct((24, hidden), F32),
        ),
        scratch_shapes=[
            pltpu.VMEM((table, width), BF16),
            pltpu.VMEM((2 * pos, width), BF16),
            pltpu.VMEM((2 * pos, width), F32),
            pltpu.VMEM((2 * pos, 2 * width), BF16),
            pltpu.VMEM((pos, width), BF16),
            pltpu.VMEM((pos, width), BF16),
            pltpu.VMEM((pos, hidden), BF16),
            pltpu.VMEM((pos, hidden), F32),
            pltpu.VMEM((pos, hidden), F32),
            pltpu.VMEM((pos, hidden), F32),
            pltpu.VMEM((pos, hidden), BF16),
            pltpu.VMEM((width, hidden), F32),
            pltpu.VMEM((hidden, hidden), F32),
        ],
        compiler_params=params,
        name="scorer",
    )(
        fetched, place.reshape(-1, 1), place.reshape(1, -1), neg_t.reshape(-1, 1), neg_t,
        w_one, b_one.reshape(1, -1), w_two, b_two.reshape(1, -1), w_out.reshape(1, -1),
    )
    received = lax.all_to_all(out, both, 0, 0, tiled=True)
    lanes = jnp.concatenate(
        [
            lists[:, :8].reshape(-1),
            jnp.pad(lists[:, 8:], ((0, 0), (0, 4)), constant_values=-1).reshape(-1),
        ]
    ).reshape(1, table)
    grad_self, grad_agg, terms = pl.pallas_call(
        owner_kernel,
        out_shape=(
            jax.ShapeDtypeStruct((nodes, width), BF16),
            jax.ShapeDtypeStruct((nodes, width), BF16),
            jax.ShapeDtypeStruct((8, 544, 128), BF16),
        ),
        scratch_shapes=[
            pltpu.VMEM((table, width), BF16),
            pltpu.VMEM((nodes, width), BF16),
            pltpu.VMEM((16, 128), F32),
        ],
        compiler_params=params,
        name="owner",
    )(received, lanes, slope, x_self, x_agg, w_self, w_nbr, scorer, bias)
    near = jnp.sum(lax.all_to_all(terms, "group", 0, 0, tiled=True).astype(F32), axis=0)
    sums = near[512:528] + near[528:544]
    far = jnp.concatenate(
        [
            near[0:384].reshape(4, 32, 3, 128).transpose(1, 0, 2, 3).reshape(32, 12, 128),
            near[384:512].reshape(2, 32, 2, 128).transpose(1, 0, 2, 3).reshape(32, 4, 128),
            jnp.broadcast_to(sums[None], (32, 16, 128)),
        ],
        axis=1,
    )
    mine = jnp.sum(lax.all_to_all(far, "inner", 0, 0, tiled=True), axis=0) / pairs
    return (
        grad_self,
        grad_agg,
        mine[0:12].reshape(4, 3, 128).transpose(1, 0, 2).reshape(-1),
        mine[12:16].reshape(2, 2, 128).transpose(1, 0, 2).reshape(-1),
        mine[16:30].reshape(-1),
    )


def solution(mesh):
    both = ("group", "inner")
    return jax.shard_map(
        body,
        mesh=mesh,
        in_specs=(
            P(both, None), P(both, None), P(), P(), P(), P(), P(), P(), P(), P(),
            P(both, None, None), P(both, None), P(both, None),
        ),
        out_specs=(P(both, None), P(both, None), P(both), P(both), P()),
        check_vma=False,
    )
```

```python
import jax
import jax.numpy as jnp
from jax import lax
from jax.experimental import pallas as pl
from jax.experimental.pallas import tpu as pltpu
from jax.sharding import PartitionSpec as P

UNROLL = 16
STEP = 32
U2 = 4
PARAMS = pltpu.CompilerParams(vmem_limit_bytes=60 * 1024 * 1024)
F32 = jnp.float32
BF16 = jnp.bfloat16


def dot(a, b):
    return jnp.dot(a, b, preferred_element_type=F32)


def dot_first(a, b):
    return lax.dot_general(a, b, (((0,), (0,)), ((), ())), preferred_element_type=F32)


def dot_last(a, b):
    return lax.dot_general(a, b, (((1,), (1,)), ((), ())), preferred_element_type=F32)


def sigm(v):
    return 0.5 + 0.5 * jnp.tanh(0.5 * v)


def one_hot(a, b):
    return jnp.where(a == b, 1.0, 0.0).astype(BF16)


def column(block, offset, period):
    count, caps = block.shape
    wide = jnp.broadcast_to(block[:, None, :], (count, 8, caps)).reshape(count * 8, caps)
    want = lax.broadcasted_iota(jnp.int32, wide.shape, 0) % period + offset
    lane = lax.broadcasted_iota(jnp.int32, wide.shape, 1)
    return jnp.sum(jnp.where(lane == want, wide, 0.0), axis=1, keepdims=True)


def layer_kernel(xs, xa, ws, wn, bl, lists, send, slope, tab):
    nodes = xs.shape[0]
    for r in range(nodes // 256):
        rows = pl.ds(r * 256, 256)
        pre = dot(xs[rows, :], ws[...]) + dot(xa[rows, :], wn[...]) + bl[...]
        s = sigm(pre)
        t = pre * s
        tab[rows, :] = t.astype(BF16)
        slope[rows, :] = s + t * (1.0 - s)
    owners = send.shape[0]
    node_ids = lax.broadcasted_iota(jnp.int32, (256, nodes), 1).astype(F32)

    def full(b, carry):
        ids = column(lists[pl.ds(b * 32, 32), :].astype(F32), 0, 8)
        y = dot(one_hot(ids, node_ids), tab[...]).astype(BF16)
        send[pl.ds(b * 32, 32), 0:8, :] = y[:, :128].reshape(32, 8, 128)
        send[pl.ds(b * 32, 32), 8:16, :] = y[:, 128:].reshape(32, 8, 128)
        return carry

    lax.fori_loop(0, owners // 32, full, 0, unroll=U2)
    low = lax.broadcasted_iota(jnp.int32, (256, 128), 0) % 8 < 4

    def mixed(b, carry):
        ids = column(lists[pl.ds(b * 32, 32), :].astype(F32), 8, 4)
        y = dot(one_hot(ids, node_ids), tab[...])
        y = jnp.where(low, y[:, :128], y[:, 128:]).astype(BF16)
        send[pl.ds(b * 32, 32), 16:24, :] = y.reshape(32, 8, 128)
        return carry

    lax.fori_loop(0, owners // 32, mixed, 0, unroll=U2)


def unpack(chunks, rows_ref):
    half = chunks.shape[0] * 8
    rows_ref[0:half, 0:128] = chunks[:, 0:8, :].reshape(half, 128)
    rows_ref[0:half, 128:256] = chunks[:, 8:16, :].reshape(half, 128)
    tail = chunks[:, 16:24, :].reshape(half, 128).astype(F32)
    rows_ref[half:, 0:128] = tail.astype(BF16)
    rows_ref[half:, 128:256] = pltpu.roll(tail, half - 4, 0).astype(BF16)


def scorer_kernel(
    chunks, pcol, plane, ncol, nlane, w1, b1, w2, b2, wo,
    out, scorer, bias,
    rows, ends, grads, split, joint, right, h1, sl1, a1, a2, d1, d2, gw1, gw2,
):
    owners = chunks.shape[0]
    table = owners * 16
    pos = ends.shape[0] // 2
    unpack(chunks, rows)
    slot_ids = lax.broadcasted_iota(jnp.int32, (256, table), 1)

    def fetch(b, carry):
        at = pl.ds(b * 256, 256)
        ends[at, :] = dot(one_hot(pcol[at, :], slot_ids), rows[...]).astype(BF16)
        return carry

    lax.fori_loop(0, 2 * pos // 256, fetch, 0, unroll=U2)
    src = ends.at[0:pos, :]
    dst = ends.at[pos : 2 * pos, :]
    grads[...] = jnp.zeros_like(grads)
    gw1[...] = jnp.zeros_like(gw1)
    gw2[...] = jnp.zeros_like(gw2)
    bias[...] = jnp.zeros_like(bias)
    step = STEP

    def block(label):
        joint[...] = (src[...].astype(F32) * right[...].astype(F32)).astype(BF16)
        a1[...] = dot(joint[...], w1[...]) + b1[...]

        def first(c, carry):
            at = pl.ds(c * step, step)
            v = a1[at, :]
            s = sigm(v)
            h = v * s
            h1[at, :] = h.astype(BF16)
            sl1[at, :] = s + h * (1.0 - s)
            return carry

        lax.fori_loop(0, pos // step, first, 0, unroll=UNROLL)
        a2[...] = dot(h1[...], w2[...]) + b2[...]

        def second(c, carry):
            sum2, sumo = carry
            at = pl.ds(c * step, step)
            v = a2[at, :]
            s = sigm(v)
            h = v * s
            score = jnp.sum(h * wo[...], axis=1, keepdims=True)
            ls = sigm(score) - label
            d = ls * wo[...] * (s + h * (1.0 - s))
            d2[at, :] = d.astype(BF16)
            return (
                sum2 + jnp.sum(d.reshape(step // 8, 8, -1), axis=0),
                sumo + jnp.sum((ls * h).reshape(step // 8, 8, -1), axis=0),
            )

        zero = jnp.zeros((8, w2.shape[1]), F32)
        sum2, sumo = lax.fori_loop(0, pos // step, second, (zero, zero), unroll=UNROLL)
        bias[8:16, :] += sum2
        bias[16:24, :] += sumo
        a1[...] = dot_last(d2[...], w2[...])

        def third(c, carry):
            at = pl.ds(c * step, step)
            d = a1[at, :] * sl1[at, :]
            d1[at, :] = d.astype(BF16)
            return carry + jnp.sum(d.reshape(step // 8, 8, -1), axis=0)

        bias[0:8, :] += lax.fori_loop(0, pos // step, third, zero, unroll=UNROLL)
        gw1[...] += dot_first(joint[...], d1[...])
        gw2[...] += dot_first(h1[...], d2[...])
        dj = dot_last(d1[...], w1[...])
        grads[0:pos, :] += dj * right[...].astype(F32)
        return dj * src[...].astype(F32)

    right[...] = dst[...]
    grads[pos:, :] += block(1.0)
    col_ids = lax.broadcasted_iota(jnp.int32, (pos, pos), 1)
    row_ids = lax.broadcasted_iota(jnp.int32, (pos, pos), 0)

    def negative(k, carry):
        right[...] = dot(one_hot(ncol[pl.ds(k * pos, pos), :], col_ids), dst[...]).astype(BF16)
        d_right = block(0.0).astype(BF16)
        grads[pos:, :] += dot(one_hot(nlane[pl.ds(k, 1), :], row_ids), d_right)
        return carry

    lax.fori_loop(0, nlane.shape[0], negative, 0)
    split[...] = grads[...].astype(BF16)
    sub = lax.broadcasted_iota(jnp.int32, (256, 2 * pos), 0)
    sub_mixed = sub - (sub & 4)

    def spread(ids):
        return dot(one_hot(plane[...], ids), split[...])

    def full(b, carry):
        y = spread(sub + b * 256).astype(BF16)
        out[pl.ds(b * 32, 32), 0:8, :] = y[:, :128].reshape(32, 8, 128)
        out[pl.ds(b * 32, 32), 8:16, :] = y[:, 128:].reshape(32, 8, 128)
        return carry

    lax.fori_loop(0, owners // 32, full, 0, unroll=U2)
    low = lax.broadcasted_iota(jnp.int32, (256, 128), 0) % 8 < 4

    def mixed(b, carry):
        y = spread(sub_mixed + (owners * 8 + b * 256))
        y = jnp.where(low, y[:, :128], y[:, 128:]).astype(BF16)
        out[pl.ds(b * 32, 32), 16:24, :] = y.reshape(32, 8, 128)
        return carry

    lax.fori_loop(0, owners // 32, mixed, 0, unroll=U2)
    for g in range(8):
        for q in range(4):
            cols = slice(q * 128, q * 128 + 128)
            lo_row = g * 96
            at = q * 96
            n1 = min(max(256 - lo_row, 0), 96)
            if n1 > 0:
                scorer[g, at : at + n1, :] = gw1[lo_row : lo_row + n1, cols].astype(BF16)
            if n1 < 96:
                first_row = lo_row + n1 - 256
                scorer[g, at + n1 : at + 96, :] = gw2[first_row : first_row + 96 - n1, cols].astype(BF16)


def owner_kernel(
    chunks, lanes, slope, xs, xa, ws, wn, bias,
    gself, gagg, terms,
    rows, dpre, sums,
):
    table = lanes.shape[1]
    nodes = xs.shape[0]
    unpack(chunks, rows)
    ids = lax.broadcasted_iota(jnp.int32, (256, table), 0)

    def nodes_step(b, carry):
        at = pl.ds(b * 256, 256)
        d = dot(one_hot(lanes[...], ids + b * 256), rows[...]) * slope[at, :]
        low = d.astype(BF16)
        dpre[at, :] = low
        gself[at, :] = dot_last(low, ws[...]).astype(BF16)
        gagg[at, :] = dot_last(low, wn[...]).astype(BF16)
        return carry + jnp.sum(d.reshape(32, 8, 256), axis=0)

    total = lax.fori_loop(0, nodes // 256, nodes_step, jnp.zeros((8, 256), F32))
    total = jnp.sum(total, axis=0, keepdims=True)
    sums[...] = jnp.zeros_like(sums)
    for part in range(3):
        whole = jnp.sum(bias[part * 8 : part * 8 + 8, :], axis=0, keepdims=True)
        for q in range(4):
            sums[part * 4 + q : part * 4 + q + 1, :] = whole[:, q * 128 : q * 128 + 128]
    for q in range(2):
        sums[12 + q : 13 + q, :] = total[:, q * 128 : q * 128 + 128]
    hi = sums[0:16, :].astype(BF16)
    lo = (sums[0:16, :] - hi.astype(F32)).astype(BF16)
    parts = (dot_first(xs[...], dpre[...]), dot_first(xa[...], dpre[...]))
    for g in range(8):
        mine = parts[g // 4]
        r = (g % 4) * 64
        for q in range(2):
            terms[g, q * 64 : q * 64 + 64, :] = mine[r : r + 64, q * 128 : q * 128 + 128].astype(BF16)
        terms[g, 128:144, :] = hi
        terms[g, 144:160, :] = lo


def call_layer(*args):
    nodes, width = args[0].shape
    owners = args[5].shape[0]
    return pl.pallas_call(
        layer_kernel,
        out_shape=(
            jax.ShapeDtypeStruct((owners, 24, 128), BF16),
            jax.ShapeDtypeStruct((nodes, width), F32),
        ),
        scratch_shapes=[pltpu.VMEM((nodes, width), BF16)],
        compiler_params=PARAMS,
        name="layer",
    )(*args)


def call_scorer(*args):
    owners = args[0].shape[0]
    pos = args[2].shape[1] // 2
    table = owners * 16
    width, hidden = args[5].shape
    return pl.pallas_call(
        scorer_kernel,
        out_shape=(
            jax.ShapeDtypeStruct((owners, 24, 128), BF16),
            jax.ShapeDtypeStruct((8, 384, 128), BF16),
            jax.ShapeDtypeStruct((24, hidden), F32),
        ),
        scratch_shapes=[
            pltpu.VMEM((table, width), BF16),
            pltpu.VMEM((2 * pos, width), BF16),
            pltpu.VMEM((2 * pos, width), F32),
            pltpu.VMEM((2 * pos, width), BF16),
            pltpu.VMEM((pos, width), BF16),
            pltpu.VMEM((pos, width), BF16),
            pltpu.VMEM((pos, hidden), BF16),
            pltpu.VMEM((pos, hidden), F32),
            pltpu.VMEM((pos, hidden), F32),
            pltpu.VMEM((pos, hidden), F32),
            pltpu.VMEM((pos, hidden), BF16),
            pltpu.VMEM((pos, hidden), BF16),
            pltpu.VMEM((width, hidden), F32),
            pltpu.VMEM((hidden, hidden), F32),
        ],
        compiler_params=PARAMS,
        name="scorer",
    )(*args)


def call_owner(*args):
    nodes, width = args[3].shape
    table = args[1].shape[1]
    return pl.pallas_call(
        owner_kernel,
        out_shape=(
            jax.ShapeDtypeStruct((nodes, width), BF16),
            jax.ShapeDtypeStruct((nodes, width), BF16),
            jax.ShapeDtypeStruct((8, 160, 128), BF16),
        ),
        scratch_shapes=[
            pltpu.VMEM((table, width), BF16),
            pltpu.VMEM((nodes, width), BF16),
            pltpu.VMEM((16, 128), F32),
        ],
        compiler_params=PARAMS,
        name="owner",
    )(*args)


def body(
    x_self, x_agg, w_self, w_nbr, b_layer, w_one, b_one, w_two, b_two, w_out,
    send_lists, endpoint_slots, neg_index,
):
    nodes, width = x_self.shape
    both = ("group", "inner")
    owners = lax.axis_size("group") * lax.axis_size("inner")
    pos = endpoint_slots.shape[0]
    negs = neg_index.shape[1]
    hidden = w_one.shape[1]
    pairs = pos * (1 + negs)
    table = owners * 16
    lists = send_lists.reshape(owners, 12)
    send, slope = call_layer(x_self, x_agg, w_self, w_nbr, b_layer.reshape(1, -1), lists)
    fetched = lax.all_to_all(send, both, 0, 0, tiled=True)
    owner = endpoint_slots // 12
    column = endpoint_slots - owner * 12
    place = jnp.where(column < 8, owner * 8 + column, owners * 8 + owner * 8 + column - 8)
    place = place.T.reshape(-1)
    neg_t = neg_index.T
    out, scorer, bias = call_scorer(
        fetched, place.reshape(-1, 1), place.reshape(1, -1), neg_t.reshape(-1, 1), neg_t,
        w_one, b_one.reshape(1, -1), w_two, b_two.reshape(1, -1), w_out.reshape(1, -1),
    )
    first = jnp.sum(lax.all_to_all(scorer, "group", 0, 0, tiled=True).astype(F32), axis=0)
    first = lax.optimization_barrier(first)
    received = lax.all_to_all(out, both, 0, 0, tiled=True)
    lanes = jnp.concatenate(
        [
            lists[:, :8].reshape(-1),
            jnp.pad(lists[:, 8:], ((0, 0), (0, 4)), constant_values=-1).reshape(-1),
        ]
    ).reshape(1, table)
    grad_self, grad_agg, terms = call_owner(
        received, lanes, slope, x_self, x_agg, w_self, w_nbr, bias
    )
    near = jnp.sum(lax.all_to_all(terms, "group", 0, 0, tiled=True).astype(F32), axis=0)
    sums = near[128:144] + near[144:160]
    far = jnp.concatenate(
        [
            first.reshape(4, 32, 3, 128).transpose(1, 0, 2, 3).reshape(32, 12, 128),
            near[0:128].reshape(2, 32, 2, 128).transpose(1, 0, 2, 3).reshape(32, 4, 128),
            jnp.broadcast_to(sums[None], (32, 16, 128)),
        ],
        axis=1,
    ).astype(BF16)
    mine = jnp.sum(lax.all_to_all(far, "inner", 0, 0, tiled=True).astype(F32), axis=0) / pairs
    return (
        grad_self,
        grad_agg,
        mine[0:12].reshape(4, 3, 128).transpose(1, 0, 2).reshape(-1),
        mine[12:16].reshape(2, 2, 128).transpose(1, 0, 2).reshape(-1),
        mine[16:30].reshape(-1),
    )


def solution(mesh):
    both = ("group", "inner")
    return jax.shard_map(
        body,
        mesh=mesh,
        in_specs=(
            P(both, None), P(both, None), P(), P(), P(), P(), P(), P(), P(), P(),
            P(both, None, None), P(both, None), P(both, None),
        ),
        out_specs=(P(both, None), P(both, None), P(both), P(both), P()),
        check_vma=False,
    )
```

```python
import jax
import jax.numpy as jnp
from jax import lax
from jax.experimental import pallas as pl
from jax.experimental.pallas import tpu as pltpu
from jax.sharding import PartitionSpec as P

UNROLL = 16
STEP = 32
U2 = 4
PARAMS = pltpu.CompilerParams(vmem_limit_bytes=36 * 1024 * 1024)
F32 = jnp.float32
BF16 = jnp.bfloat16


def dot(a, b):
    return jnp.dot(a, b, preferred_element_type=F32)


def dot_first(a, b):
    return lax.dot_general(a, b, (((0,), (0,)), ((), ())), preferred_element_type=F32)


def dot_last(a, b):
    return lax.dot_general(a, b, (((1,), (1,)), ((), ())), preferred_element_type=F32)


def sigm(v):
    return 0.5 + 0.5 * jnp.tanh(0.5 * v)


def one_hot(a, b):
    return jnp.where(a == b, 1.0, 0.0).astype(BF16)


def column(block, offset, period):
    count, caps = block.shape
    wide = jnp.broadcast_to(block[:, None, :], (count, 8, caps)).reshape(count * 8, caps)
    want = lax.broadcasted_iota(jnp.int32, wide.shape, 0) % period + offset
    lane = lax.broadcasted_iota(jnp.int32, wide.shape, 1)
    return jnp.sum(jnp.where(lane == want, wide, 0.0), axis=1, keepdims=True)


def layer_kernel(xs, xa, ws, wn, bl, lists, send, slope, tab):
    nodes = xs.shape[0]
    for r in range(nodes // 256):
        rows = pl.ds(r * 256, 256)
        pre = dot(xs[rows, :], ws[...]) + dot(xa[rows, :], wn[...]) + bl[...]
        s = sigm(pre)
        t = pre * s
        tab[rows, :] = t.astype(BF16)
        slope[rows, :] = s + t * (1.0 - s)
    owners = send.shape[0]
    node_ids = lax.broadcasted_iota(jnp.int32, (256, nodes), 1).astype(F32)

    low = lax.broadcasted_iota(jnp.int32, (256, 128), 0) % 8 < 4
    for b in range(owners // 32):
        mine = jnp.transpose(lists[:, b, :].astype(F32))
        at = slice(b * 32, b * 32 + 32)
        y = dot(one_hot(column(mine, 0, 8), node_ids), tab[...]).astype(BF16)
        send[at, 0:8, :] = y[:, :128].reshape(32, 8, 128)
        send[at, 8:16, :] = y[:, 128:].reshape(32, 8, 128)
        y = dot(one_hot(column(mine, 8, 4), node_ids), tab[...])
        y = jnp.where(low, y[:, :128], y[:, 128:]).astype(BF16)
        send[at, 16:24, :] = y.reshape(32, 8, 128)


def unpack(chunks, rows_ref):
    half = chunks.shape[0] * 8
    rows_ref[0:half, 0:128] = chunks[:, 0:8, :].reshape(half, 128)
    rows_ref[0:half, 128:256] = chunks[:, 8:16, :].reshape(half, 128)
    tail = chunks[:, 16:24, :].reshape(half, 128).astype(F32)
    rows_ref[half:, 0:128] = tail.astype(BF16)
    rows_ref[half:, 128:256] = pltpu.roll(tail, half - 4, 0).astype(BF16)


def pair_blocks(ends, right, joint, h1, sl1, a1, a2, d1, d2, ncol, nlane, w1, b1, w2, b2, wo, grads, gw1, gw2, bias):
    pos = ends.shape[0] // 2
    src = ends.at[0:pos, :]
    dst = ends.at[pos : 2 * pos, :]

    def block(label):
        joint[...] = (src[...].astype(F32) * right[...].astype(F32)).astype(BF16)
        a1[...] = dot(joint[...], w1[...]) + b1[...]

        def first(c, carry):
            at = pl.ds(c * STEP, STEP)
            v = a1[at, :]
            s = sigm(v)
            h = v * s
            h1[at, :] = h.astype(BF16)
            sl1[at, :] = s + h * (1.0 - s)
            return carry

        lax.fori_loop(0, pos // STEP, first, 0, unroll=UNROLL)
        a2[...] = dot(h1[...], w2[...]) + b2[...]
        zero = jnp.zeros((8, w2.shape[1]), F32)

        def fold(d):
            return jnp.sum(d.reshape(STEP // 8, 8, -1), axis=0)

        def second(c, carry):
            at = pl.ds(c * STEP, STEP)
            v = a2[at, :]
            s = sigm(v)
            h = v * s
            score = jnp.sum(h * wo[...], axis=1, keepdims=True)
            ls = sigm(score) - label
            d = ls * wo[...] * (s + h * (1.0 - s))
            d2[at, :] = d.astype(BF16)
            if grads is not None:
                return carry
            return (carry[0] + fold(d), carry[1] + fold(ls * h))

        start = 0 if grads is not None else (zero, zero)
        sums = lax.fori_loop(0, pos // STEP, second, start, unroll=UNROLL)
        a1[...] = dot_last(d2[...], w2[...])

        def third(c, carry):
            at = pl.ds(c * STEP, STEP)
            d = a1[at, :] * sl1[at, :]
            d1[at, :] = d.astype(BF16)
            return carry if grads is not None else carry + fold(d)

        start = 0 if grads is not None else zero
        sum1 = lax.fori_loop(0, pos // STEP, third, start, unroll=UNROLL)
        if grads is None:
            bias[0:8, :] += sum1
            bias[8:16, :] += sums[0]
            bias[16:24, :] += sums[1]
            gw1[...] += dot_first(joint[...], d1[...])
            gw2[...] += dot_first(h1[...], d2[...])
            return None
        dj = dot_last(d1[...], w1[...])
        grads[0:pos, :] += dj * right[...].astype(F32)
        return dj * src[...].astype(F32)

    right[...] = dst[...]
    d_right = block(1.0)
    if grads is not None:
        grads[pos:, :] += d_right
    col_ids = lax.broadcasted_iota(jnp.int32, (pos, pos), 1)
    row_ids = lax.broadcasted_iota(jnp.int32, (pos, pos), 0)

    def negative(k, carry):
        right[...] = dot(one_hot(ncol[pl.ds(k * pos, pos), :], col_ids), dst[...]).astype(BF16)
        d_right = block(0.0)
        if grads is not None:
            grads[pos:, :] += dot(one_hot(nlane[pl.ds(k, 1), :], row_ids), d_right.astype(BF16))
        return carry

    lax.fori_loop(0, ncol.shape[0] // pos, negative, 0)


def slots_kernel(
    chunks, pcol, plane, ncol, nlane, w1, b1, w2, b2, wo,
    out, ends,
    rows, grads, split, right, joint, h1, sl1, a1, a2, d1, d2,
):
    owners = chunks.shape[0]
    table = owners * 16
    pos = ends.shape[0] // 2
    unpack(chunks, rows)
    slot_ids = lax.broadcasted_iota(jnp.int32, (256, table), 1)

    def fetch(b, carry):
        at = pl.ds(b * 256, 256)
        ends[at, :] = dot(one_hot(pcol[at, :], slot_ids), rows[...]).astype(BF16)
        return carry

    lax.fori_loop(0, 2 * pos // 256, fetch, 0, unroll=U2)
    grads[...] = jnp.zeros_like(grads)
    pair_blocks(
        ends, right, joint, h1, sl1, a1, a2, d1, d2, ncol, nlane, w1, b1, w2, b2, wo, grads, None, None, None
    )
    split[...] = grads[...].astype(BF16)
    sub = lax.broadcasted_iota(jnp.int32, (256, 2 * pos), 0)
    sub_mixed = sub - (sub & 4)

    def spread(ids):
        return dot(one_hot(plane[...], ids), split[...])

    def full(b, carry):
        y = spread(sub + b * 256).astype(BF16)
        out[pl.ds(b * 32, 32), 0:8, :] = y[:, :128].reshape(32, 8, 128)
        out[pl.ds(b * 32, 32), 8:16, :] = y[:, 128:].reshape(32, 8, 128)
        return carry

    lax.fori_loop(0, owners // 32, full, 0, unroll=U2)
    low = lax.broadcasted_iota(jnp.int32, (256, 128), 0) % 8 < 4

    def mixed(b, carry):
        y = spread(sub_mixed + (owners * 8 + b * 256))
        y = jnp.where(low, y[:, :128], y[:, 128:]).astype(BF16)
        out[pl.ds(b * 32, 32), 16:24, :] = y.reshape(32, 8, 128)
        return carry

    lax.fori_loop(0, owners // 32, mixed, 0, unroll=U2)


def weights_kernel(
    ends, ncol, w1, b1, w2, b2, wo,
    scorer, bias,
    right, joint, h1, sl1, a1, a2, d1, d2, gw1, gw2,
):
    gw1[...] = jnp.zeros_like(gw1)
    gw2[...] = jnp.zeros_like(gw2)
    bias[...] = jnp.zeros_like(bias)
    pair_blocks(
        ends, right, joint, h1, sl1, a1, a2, d1, d2, ncol, None, w1, b1, w2, b2, wo, None, gw1, gw2, bias
    )
    for g in range(8):
        for q in range(4):
            cols = slice(q * 128, q * 128 + 128)
            lo_row = g * 96
            at = q * 96
            n1 = min(max(256 - lo_row, 0), 96)
            if n1 > 0:
                scorer[g, at : at + n1, :] = gw1[lo_row : lo_row + n1, cols].astype(BF16)
            if n1 < 96:
                first_row = lo_row + n1 - 256
                scorer[g, at + n1 : at + 96, :] = gw2[first_row : first_row + 96 - n1, cols].astype(BF16)


def owner_kernel(
    chunks, lanes, slope, xs, xa, bias,
    dpre, terms,
    rows, sums,
):
    table = lanes.shape[1]
    nodes = xs.shape[0]
    unpack(chunks, rows)
    ids = lax.broadcasted_iota(jnp.int32, (256, table), 0)

    def nodes_step(b, carry):
        at = pl.ds(b * 256, 256)
        d = dot(one_hot(lanes[...], ids + b * 256), rows[...]) * slope[at, :]
        low = d.astype(BF16)
        dpre[at, :] = low
        return carry + jnp.sum(d.reshape(32, 8, 256), axis=0)

    total = lax.fori_loop(0, nodes // 256, nodes_step, jnp.zeros((8, 256), F32))
    total = jnp.sum(total, axis=0, keepdims=True)
    sums[...] = jnp.zeros_like(sums)
    for part in range(3):
        whole = jnp.sum(bias[part * 8 : part * 8 + 8, :], axis=0, keepdims=True)
        for q in range(4):
            sums[part * 4 + q : part * 4 + q + 1, :] = whole[:, q * 128 : q * 128 + 128]
    for q in range(2):
        sums[12 + q : 13 + q, :] = total[:, q * 128 : q * 128 + 128]
    hi = sums[0:16, :].astype(BF16)
    lo = (sums[0:16, :] - hi.astype(F32)).astype(BF16)
    parts = (dot_first(xs[...], dpre[...]), dot_first(xa[...], dpre[...]))
    for g in range(8):
        mine = parts[g // 4]
        r = (g % 4) * 64
        for q in range(2):
            terms[g, q * 64 : q * 64 + 64, :] = mine[r : r + 64, q * 128 : q * 128 + 128].astype(BF16)
        terms[g, 128:144, :] = hi
        terms[g, 144:160, :] = lo


def inputs_kernel(dpre, ws, wn, gself, gagg):
    gself[...] = dot_last(dpre[...], ws[...]).astype(BF16)
    gagg[...] = dot_last(dpre[...], wn[...]).astype(BF16)


def call_layer(*args):
    nodes, width = args[0].shape
    owners = args[5].shape[1] * args[5].shape[2]
    return pl.pallas_call(
        layer_kernel,
        out_shape=(
            jax.ShapeDtypeStruct((owners, 24, 128), BF16),
            jax.ShapeDtypeStruct((nodes, width), F32),
        ),
        scratch_shapes=[pltpu.VMEM((nodes, width), BF16)],
        compiler_params=PARAMS,
        name="layer",
    )(*args)


def block_scratch(pos, width, hidden):
    return [
        pltpu.VMEM((pos, width), BF16),
        pltpu.VMEM((pos, width), BF16),
        pltpu.VMEM((pos, hidden), BF16),
        pltpu.VMEM((pos, hidden), F32),
        pltpu.VMEM((pos, hidden), F32),
        pltpu.VMEM((pos, hidden), F32),
        pltpu.VMEM((pos, hidden), BF16),
        pltpu.VMEM((pos, hidden), BF16),
    ]


def call_slots(*args):
    owners = args[0].shape[0]
    pos = args[2].shape[1] // 2
    width, hidden = args[5].shape
    return pl.pallas_call(
        slots_kernel,
        out_shape=(
            jax.ShapeDtypeStruct((owners, 24, 128), BF16),
            jax.ShapeDtypeStruct((2 * pos, width), BF16),
        ),
        scratch_shapes=[
            pltpu.VMEM((owners * 16, width), BF16),
            pltpu.VMEM((2 * pos, width), F32),
            pltpu.VMEM((2 * pos, width), BF16),
        ]
        + block_scratch(pos, width, hidden),
        compiler_params=PARAMS,
        name="slots",
    )(*args)


def call_weights(*args):
    pos = args[0].shape[0] // 2
    width, hidden = args[2].shape
    return pl.pallas_call(
        weights_kernel,
        out_shape=(
            jax.ShapeDtypeStruct((8, 384, 128), BF16),
            jax.ShapeDtypeStruct((24, hidden), F32),
        ),
        scratch_shapes=block_scratch(pos, width, hidden)
        + [pltpu.VMEM((width, hidden), F32), pltpu.VMEM((hidden, hidden), F32)],
        compiler_params=PARAMS,
        name="weights",
    )(*args)


def call_owner(*args):
    nodes, width = args[3].shape
    table = args[1].shape[1]
    return pl.pallas_call(
        owner_kernel,
        out_shape=(
            jax.ShapeDtypeStruct((nodes, width), BF16),
            jax.ShapeDtypeStruct((8, 160, 128), BF16),
        ),
        scratch_shapes=[pltpu.VMEM((table, width), BF16), pltpu.VMEM((16, 128), F32)],
        compiler_params=PARAMS,
        name="owner",
    )(*args)


def call_inputs(*args):
    return pl.pallas_call(
        inputs_kernel,
        out_shape=(
            jax.ShapeDtypeStruct(args[0].shape, BF16),
            jax.ShapeDtypeStruct(args[0].shape, BF16),
        ),
        compiler_params=PARAMS,
        name="inputs",
    )(*args)


def near_core(x):
    return pltpu.with_memory_space_constraint(x, pltpu.VMEM)


def body(
    x_self, x_agg, w_self, w_nbr, b_layer, w_one, b_one, w_two, b_two, w_out,
    send_lists, endpoint_slots, neg_index,
):
    nodes, width = x_self.shape
    both = ("group", "inner")
    owners = lax.axis_size("group") * lax.axis_size("inner")
    pos = endpoint_slots.shape[0]
    negs = neg_index.shape[1]
    hidden = w_one.shape[1]
    pairs = pos * (1 + negs)
    table = owners * 16
    lists = send_lists.reshape(owners, 12)
    send, slope = call_layer(x_self, x_agg, w_self, w_nbr, b_layer.reshape(1, -1), send_lists.transpose(2, 0, 1))
    fetched = near_core(lax.all_to_all(send, both, 0, 0, tiled=True))
    owner = endpoint_slots // 12
    column = endpoint_slots - owner * 12
    place = jnp.where(column < 8, owner * 8 + column, owners * 8 + owner * 8 + column - 8)
    place = place.T.reshape(-1)
    neg_t = neg_index.T
    ncol = neg_t.reshape(-1, 1)
    scorer_args = (w_one, b_one.reshape(1, -1), w_two, b_two.reshape(1, -1), w_out.reshape(1, -1))
    out, ends = call_slots(fetched, place.reshape(-1, 1), place.reshape(1, -1), ncol, neg_t, *scorer_args)
    scorer, bias = call_weights(ends, ncol, *scorer_args)
    first = jnp.sum(lax.all_to_all(scorer, "group", 0, 0, tiled=True).astype(F32), axis=0)
    first = lax.optimization_barrier(first)
    received = near_core(lax.all_to_all(out, both, 0, 0, tiled=True))
    lanes = jnp.concatenate(
        [
            lists[:, :8].reshape(-1),
            jnp.pad(lists[:, 8:], ((0, 0), (0, 4)), constant_values=-1).reshape(-1),
        ]
    ).reshape(1, table)
    d_pre, terms = call_owner(received, lanes, slope, x_self, x_agg, bias)
    grad_self, grad_agg = call_inputs(d_pre, w_self, w_nbr)
    near = jnp.sum(lax.all_to_all(terms, "group", 0, 0, tiled=True).astype(F32), axis=0)
    sums = near[128:144] + near[144:160]
    far = jnp.concatenate(
        [
            first.reshape(4, 32, 3, 128).transpose(1, 0, 2, 3).reshape(32, 12, 128),
            near[0:128].reshape(2, 32, 2, 128).transpose(1, 0, 2, 3).reshape(32, 4, 128),
            jnp.broadcast_to(sums[None], (32, 16, 128)),
        ],
        axis=1,
    ).astype(BF16)
    mine = jnp.sum(lax.all_to_all(far, "inner", 0, 0, tiled=True).astype(F32), axis=0) / pairs
    return (
        grad_self,
        grad_agg,
        mine[0:12].reshape(4, 3, 128).transpose(1, 0, 2).reshape(-1),
        mine[12:16].reshape(2, 2, 128).transpose(1, 0, 2).reshape(-1),
        mine[16:30].reshape(-1),
    )


def solution(mesh):
    both = ("group", "inner")
    return jax.shard_map(
        body,
        mesh=mesh,
        in_specs=(
            P(both, None), P(both, None), P(), P(), P(), P(), P(), P(), P(), P(),
            P(both, None, None), P(both, None), P(both, None),
        ),
        out_specs=(P(both, None), P(both, None), P(both), P(both), P()),
        check_vma=False,
    )
```

```python
import jax
import jax.numpy as jnp
from jax import lax
from jax.experimental import pallas as pl
from jax.experimental.pallas import tpu as pltpu
from jax.sharding import PartitionSpec as P

UNROLL = 16
STEP = 32
U2 = 4
PARAMS = pltpu.CompilerParams(vmem_limit_bytes=36 * 1024 * 1024)
WIDE = pltpu.CompilerParams(vmem_limit_bytes=60 * 1024 * 1024)
F32 = jnp.float32
BF16 = jnp.bfloat16


def dot(a, b):
    return jnp.dot(a, b, preferred_element_type=F32)


def dot_first(a, b):
    return lax.dot_general(a, b, (((0,), (0,)), ((), ())), preferred_element_type=F32)


def dot_last(a, b):
    return lax.dot_general(a, b, (((1,), (1,)), ((), ())), preferred_element_type=F32)


def sigm(v):
    return 0.5 + 0.5 * jnp.tanh(0.5 * v)


def one_hot(a, b):
    return jnp.where(a == b, 1.0, 0.0).astype(BF16)


def column(block, offset, period):
    count, caps = block.shape
    wide = jnp.broadcast_to(block[:, None, :], (count, 8, caps)).reshape(count * 8, caps)
    want = lax.broadcasted_iota(jnp.int32, wide.shape, 0) % period + offset
    lane = lax.broadcasted_iota(jnp.int32, wide.shape, 1)
    return jnp.sum(jnp.where(lane == want, wide, 0.0), axis=1, keepdims=True)


def layer_kernel(far_xs, far_xa, ws, wn, bl, lists, sent, far_slope, xs, xa, slope, tab, send, sems, loads, saves):
    nodes = xs.shape[0]
    steps = nodes // 256

    def load(r, k):
        rows = pl.ds(r * 256, 256)
        far, near = ((far_xs, xs), (far_xa, xa))[k]
        return pltpu.make_async_copy(far.at[rows], near.at[rows], loads.at[k, r])

    def save(r):
        rows = pl.ds(r * 256, 256)
        return pltpu.make_async_copy(slope.at[rows], far_slope.at[rows], saves.at[r])

    for r in range(steps):
        load(r, 0).start()
        load(r, 1).start()
    for r in range(steps):
        rows = pl.ds(r * 256, 256)
        load(r, 0).wait()
        load(r, 1).wait()
        pre = dot(xs[rows, :], ws[...]) + dot(xa[rows, :], wn[...]) + bl[...]
        s = sigm(pre)
        t = pre * s
        tab[rows, :] = t.astype(BF16)
        slope[rows, :] = s + t * (1.0 - s)
        save(r).start()
    owners = send.shape[0]
    copies = []
    node_ids = lax.broadcasted_iota(jnp.int32, (256, nodes), 1).astype(F32)

    low = lax.broadcasted_iota(jnp.int32, (256, 128), 0) % 8 < 4
    for b in range(owners // 32):
        mine = jnp.transpose(lists[:, b, :].astype(F32))
        at = slice(b * 32, b * 32 + 32)
        y = dot(one_hot(column(mine, 0, 8), node_ids), tab[...]).astype(BF16)
        send[at, 0:8, :] = y[:, :128].reshape(32, 8, 128)
        send[at, 8:16, :] = y[:, 128:].reshape(32, 8, 128)
        y = dot(one_hot(column(mine, 8, 4), node_ids), tab[...])
        y = jnp.where(low, y[:, :128], y[:, 128:]).astype(BF16)
        send[at, 16:24, :] = y.reshape(32, 8, 128)
        copies.append(pltpu.make_async_copy(send.at[pl.ds(b * 32, 32)], sent.at[pl.ds(b * 32, 32)], sems.at[b]))
        copies[-1].start()
    for copy in copies:
        copy.wait()
    for r in range(steps):
        save(r).wait()


def unpack(chunks, rows_ref):
    half = chunks.shape[0] * 8
    rows_ref[0:half, 0:128] = chunks[:, 0:8, :].reshape(half, 128)
    rows_ref[0:half, 128:256] = chunks[:, 8:16, :].reshape(half, 128)
    tail = chunks[:, 16:24, :].reshape(half, 128).astype(F32)
    rows_ref[half:, 0:128] = tail.astype(BF16)
    rows_ref[half:, 128:256] = pltpu.roll(tail, half - 4, 0).astype(BF16)


def pair_blocks(ends, right, joint, h1, sl1, a1, a2, d1, d2, ncol, nlane, w1, b1, w2, b2, wo, grads, gw1, gw2, bias):
    pos = ends.shape[0] // 2
    src = ends.at[0:pos, :]
    dst = ends.at[pos : 2 * pos, :]

    def block(label):
        joint[...] = (src[...].astype(F32) * right[...].astype(F32)).astype(BF16)
        a1[...] = dot(joint[...], w1[...]) + b1[...]

        def first(c, carry):
            at = pl.ds(c * STEP, STEP)
            v = a1[at, :]
            s = sigm(v)
            h = v * s
            h1[at, :] = h.astype(BF16)
            sl1[at, :] = s + h * (1.0 - s)
            return carry

        lax.fori_loop(0, pos // STEP, first, 0, unroll=UNROLL)
        a2[...] = dot(h1[...], w2[...]) + b2[...]
        zero = jnp.zeros((8, w2.shape[1]), F32)

        def fold(d):
            return jnp.sum(d.reshape(STEP // 8, 8, -1), axis=0)

        def second(c, carry):
            at = pl.ds(c * STEP, STEP)
            v = a2[at, :]
            s = sigm(v)
            h = v * s
            score = jnp.sum(h * wo[...], axis=1, keepdims=True)
            ls = sigm(score) - label
            d = ls * wo[...] * (s + h * (1.0 - s))
            d2[at, :] = d.astype(BF16)
            if grads is not None:
                return carry
            return (carry[0] + fold(d), carry[1] + fold(ls * h))

        start = 0 if grads is not None else (zero, zero)
        sums = lax.fori_loop(0, pos // STEP, second, start, unroll=UNROLL)
        a1[...] = dot_last(d2[...], w2[...])

        def third(c, carry):
            at = pl.ds(c * STEP, STEP)
            d = a1[at, :] * sl1[at, :]
            d1[at, :] = d.astype(BF16)
            return carry if grads is not None else carry + fold(d)

        start = 0 if grads is not None else zero
        sum1 = lax.fori_loop(0, pos // STEP, third, start, unroll=UNROLL)
        if grads is None:
            bias[0:8, :] += sum1
            bias[8:16, :] += sums[0]
            bias[16:24, :] += sums[1]
            gw1[...] += dot_first(joint[...], d1[...])
            gw2[...] += dot_first(h1[...], d2[...])
            return None
        dj = dot_last(d1[...], w1[...])
        grads[0:pos, :] += dj * right[...].astype(F32)
        return dj * src[...].astype(F32)

    right[...] = dst[...]
    d_right = block(1.0)
    if grads is not None:
        grads[pos:, :] += d_right
    col_ids = lax.broadcasted_iota(jnp.int32, (pos, pos), 1)
    row_ids = lax.broadcasted_iota(jnp.int32, (pos, pos), 0)

    def negative(k, carry):
        right[...] = dot(one_hot(ncol[pl.ds(k * pos, pos), :], col_ids), dst[...]).astype(BF16)
        d_right = block(0.0)
        if grads is not None:
            grads[pos:, :] += dot(one_hot(nlane[pl.ds(k, 1), :], row_ids), d_right.astype(BF16))
        return carry

    lax.fori_loop(0, ncol.shape[0] // pos, negative, 0)


def slots_kernel(
    chunks, pcol, plane, ncol, nlane, far_w1, b1, far_w2, b2, wo,
    sent, far_ends,
    rows, grads, split, out, sems, ends, w1, w2, others, right, joint, h1, sl1, a1, a2, d1, d2,
):
    owners = chunks.shape[0]
    table = owners * 16
    pos = ends.shape[0] // 2
    load_w1 = pltpu.make_async_copy(far_w1, w1, others.at[0])
    load_w2 = pltpu.make_async_copy(far_w2, w2, others.at[1])
    load_w1.start()
    load_w2.start()
    unpack(chunks, rows)
    slot_ids = lax.broadcasted_iota(jnp.int32, (256, table), 1)

    def fetch(b, carry):
        at = pl.ds(b * 256, 256)
        ends[at, :] = dot(one_hot(pcol[at, :], slot_ids), rows[...]).astype(BF16)
        return carry

    lax.fori_loop(0, 2 * pos // 256, fetch, 0, unroll=U2)
    save_ends = pltpu.make_async_copy(ends, far_ends, others.at[2])
    save_ends.start()
    load_w1.wait()
    load_w2.wait()
    grads[...] = jnp.zeros_like(grads)
    pair_blocks(
        ends, right, joint, h1, sl1, a1, a2, d1, d2, ncol, nlane, w1, b1, w2, b2, wo, grads, None, None, None
    )
    split[...] = grads[...].astype(BF16)
    sub = lax.broadcasted_iota(jnp.int32, (256, 2 * pos), 0)
    sub_mixed = sub - (sub & 4)

    def spread(ids):
        return dot(one_hot(plane[...], ids), split[...])

    low = lax.broadcasted_iota(jnp.int32, (256, 128), 0) % 8 < 4
    copies = []
    for b in range(owners // 32):
        at = slice(b * 32, b * 32 + 32)
        y = spread(sub + b * 256).astype(BF16)
        out[at, 0:8, :] = y[:, :128].reshape(32, 8, 128)
        out[at, 8:16, :] = y[:, 128:].reshape(32, 8, 128)
        y = spread(sub_mixed + (owners * 8 + b * 256))
        y = jnp.where(low, y[:, :128], y[:, 128:]).astype(BF16)
        out[at, 16:24, :] = y.reshape(32, 8, 128)
        copies.append(pltpu.make_async_copy(out.at[pl.ds(b * 32, 32)], sent.at[pl.ds(b * 32, 32)], sems.at[b]))
        copies[-1].start()
    for copy in copies:
        copy.wait()
    save_ends.wait()


def weights_kernel(
    ends, ncol, w1, b1, w2, b2, wo,
    scorer, bias,
    right, joint, h1, sl1, a1, a2, d1, d2, gw1, gw2,
):
    gw1[...] = jnp.zeros_like(gw1)
    gw2[...] = jnp.zeros_like(gw2)
    bias[...] = jnp.zeros_like(bias)
    pair_blocks(
        ends, right, joint, h1, sl1, a1, a2, d1, d2, ncol, None, w1, b1, w2, b2, wo, None, gw1, gw2, bias
    )
    for g in range(8):
        for q in range(4):
            cols = slice(q * 128, q * 128 + 128)
            lo_row = g * 96
            at = q * 96
            n1 = min(max(256 - lo_row, 0), 96)
            if n1 > 0:
                scorer[g, at : at + n1, :] = gw1[lo_row : lo_row + n1, cols].astype(BF16)
            if n1 < 96:
                first_row = lo_row + n1 - 256
                scorer[g, at + n1 : at + 96, :] = gw2[first_row : first_row + 96 - n1, cols].astype(BF16)


def owner_kernel(
    chunks, lanes, far_slope, xs, xa, bias,
    dpre, terms,
    rows, sums, slope, sem,
):
    table = lanes.shape[1]
    nodes = xs.shape[0]
    load = pltpu.make_async_copy(far_slope, slope, sem.at[0])
    load.start()
    unpack(chunks, rows)
    load.wait()
    ids = lax.broadcasted_iota(jnp.int32, (256, table), 0)

    def nodes_step(b, carry):
        at = pl.ds(b * 256, 256)
        d = dot(one_hot(lanes[...], ids + b * 256), rows[...]) * slope[at, :]
        low = d.astype(BF16)
        dpre[at, :] = low
        return carry + jnp.sum(d.reshape(32, 8, 256), axis=0)

    total = lax.fori_loop(0, nodes // 256, nodes_step, jnp.zeros((8, 256), F32))
    total = jnp.sum(total, axis=0, keepdims=True)
    sums[...] = jnp.zeros_like(sums)
    for part in range(3):
        whole = jnp.sum(bias[part * 8 : part * 8 + 8, :], axis=0, keepdims=True)
        for q in range(4):
            sums[part * 4 + q : part * 4 + q + 1, :] = whole[:, q * 128 : q * 128 + 128]
    for q in range(2):
        sums[12 + q : 13 + q, :] = total[:, q * 128 : q * 128 + 128]
    hi = sums[0:16, :].astype(BF16)
    lo = (sums[0:16, :] - hi.astype(F32)).astype(BF16)
    parts = (dot_first(xs[...], dpre[...]), dot_first(xa[...], dpre[...]))
    for g in range(8):
        mine = parts[g // 4]
        r = (g % 4) * 64
        for q in range(2):
            terms[g, q * 64 : q * 64 + 64, :] = mine[r : r + 64, q * 128 : q * 128 + 128].astype(BF16)
        terms[g, 128:144, :] = hi
        terms[g, 144:160, :] = lo


def inputs_kernel(dpre, ws, wn, gself, gagg):
    gself[...] = dot_last(dpre[...], ws[...]).astype(BF16)
    gagg[...] = dot_last(dpre[...], wn[...]).astype(BF16)


def call_layer(*args):
    nodes, width = args[0].shape
    owners = args[5].shape[1] * args[5].shape[2]
    return pl.pallas_call(
        layer_kernel,
        out_shape=(
            pltpu.HBM((owners, 24, 128), BF16),
            pltpu.HBM((nodes, width), F32),
        ),
        in_specs=[pl.BlockSpec(memory_space=pltpu.HBM)] * 2 + [pl.BlockSpec(memory_space=pltpu.VMEM)] * 4,
        out_specs=(pl.BlockSpec(memory_space=pltpu.HBM), pl.BlockSpec(memory_space=pltpu.HBM)),
        scratch_shapes=[
            pltpu.VMEM((nodes, width), BF16),
            pltpu.VMEM((nodes, width), BF16),
            pltpu.VMEM((nodes, width), F32),
            pltpu.VMEM((nodes, width), BF16),
            pltpu.VMEM((owners, 24, 128), BF16),
            pltpu.SemaphoreType.DMA((owners // 32,)),
            pltpu.SemaphoreType.DMA((2, nodes // 256)),
            pltpu.SemaphoreType.DMA((nodes // 256,)),
        ],
        compiler_params=WIDE,
        name="layer",
    )(*args)


def block_scratch(pos, width, hidden):
    return [
        pltpu.VMEM((pos, width), BF16),
        pltpu.VMEM((pos, width), BF16),
        pltpu.VMEM((pos, hidden), BF16),
        pltpu.VMEM((pos, hidden), F32),
        pltpu.VMEM((pos, hidden), F32),
        pltpu.VMEM((pos, hidden), F32),
        pltpu.VMEM((pos, hidden), BF16),
        pltpu.VMEM((pos, hidden), BF16),
    ]


def call_slots(*args):
    owners = args[0].shape[0]
    pos = args[2].shape[1] // 2
    width, hidden = args[5].shape
    return pl.pallas_call(
        slots_kernel,
        out_shape=(
            pltpu.HBM((owners, 24, 128), BF16),
            pltpu.HBM((2 * pos, width), BF16),
        ),
        in_specs=[pl.BlockSpec(memory_space=pltpu.HBM if k in (5, 7) else pltpu.VMEM) for k in range(10)],
        out_specs=(pl.BlockSpec(memory_space=pltpu.HBM), pl.BlockSpec(memory_space=pltpu.HBM)),
        scratch_shapes=[
            pltpu.VMEM((owners * 16, width), BF16),
            pltpu.VMEM((2 * pos, width), F32),
            pltpu.VMEM((2 * pos, width), BF16),
            pltpu.VMEM((owners, 24, 128), BF16),
            pltpu.SemaphoreType.DMA((owners // 32,)),
            pltpu.VMEM((2 * pos, width), BF16),
            pltpu.VMEM((width, hidden), BF16),
            pltpu.VMEM((hidden, hidden), BF16),
            pltpu.SemaphoreType.DMA((3,)),
        ]
        + block_scratch(pos, width, hidden),
        compiler_params=PARAMS,
        name="slots",
    )(*args)


def call_weights(*args):
    pos = args[0].shape[0] // 2
    width, hidden = args[2].shape
    return pl.pallas_call(
        weights_kernel,
        out_shape=(
            jax.ShapeDtypeStruct((8, 384, 128), BF16),
            jax.ShapeDtypeStruct((24, hidden), F32),
        ),
        scratch_shapes=block_scratch(pos, width, hidden)
        + [pltpu.VMEM((width, hidden), F32), pltpu.VMEM((hidden, hidden), F32)],
        compiler_params=PARAMS,
        name="weights",
    )(*args)


def call_owner(*args):
    nodes, width = args[3].shape
    table = args[1].shape[1]
    return pl.pallas_call(
        owner_kernel,
        out_shape=(
            jax.ShapeDtypeStruct((nodes, width), BF16),
            pltpu.HBM((8, 160, 128), BF16),
        ),
        in_specs=[pl.BlockSpec(memory_space=pltpu.HBM if k == 2 else pltpu.VMEM) for k in range(6)],
        scratch_shapes=[
            pltpu.VMEM((table, width), BF16),
            pltpu.VMEM((16, 128), F32),
            pltpu.VMEM((nodes, width), F32),
            pltpu.SemaphoreType.DMA((1,)),
        ],
        compiler_params=PARAMS,
        name="owner",
    )(*args)


def call_inputs(*args):
    return pl.pallas_call(
        inputs_kernel,
        out_shape=(
            jax.ShapeDtypeStruct(args[0].shape, BF16),
            jax.ShapeDtypeStruct(args[0].shape, BF16),
        ),
        compiler_params=PARAMS,
        name="inputs",
    )(*args)


def far_core(x):
    return pltpu.with_memory_space_constraint(x, pltpu.HBM)


def near_core(x):
    return pltpu.with_memory_space_constraint(x, pltpu.VMEM)


def body(
    x_self, x_agg, w_self, w_nbr, b_layer, w_one, b_one, w_two, b_two, w_out,
    send_lists, endpoint_slots, neg_index,
):
    both = ("group", "inner")
    owners = lax.axis_size("group") * lax.axis_size("inner")
    pos = endpoint_slots.shape[0]
    negs = neg_index.shape[1]
    pairs = pos * (1 + negs)
    table = owners * 16
    lists = send_lists.reshape(owners, 12)
    send, slope = call_layer(far_core(x_self), far_core(x_agg), w_self, w_nbr, b_layer.reshape(1, -1), send_lists.transpose(2, 0, 1))
    w_one_far, w_two_far = far_core(w_one), far_core(w_two)
    fetched = near_core(lax.all_to_all(send, both, 0, 0, tiled=True))
    owner = endpoint_slots // 12
    column = endpoint_slots - owner * 12
    place = jnp.where(column < 8, owner * 8 + column, owners * 8 + owner * 8 + column - 8)
    place = place.T.reshape(-1)
    neg_t = neg_index.T
    ncol = neg_t.reshape(-1, 1)
    scorer_args = (w_one, b_one.reshape(1, -1), w_two, b_two.reshape(1, -1), w_out.reshape(1, -1))
    out, ends = call_slots(fetched, place.reshape(-1, 1), place.reshape(1, -1), ncol, neg_t, w_one_far, scorer_args[1], w_two_far, *scorer_args[3:])
    scorer, bias = call_weights(ends, ncol, *scorer_args)
    groups = lax.axis_size("group")
    here = lax.axis_index("group")
    pieces = [lax.dynamic_index_in_dim(scorer, here, 0, False).astype(F32)]
    for k in range(1, groups):
        piece = lax.dynamic_index_in_dim(scorer, (here + k) % groups, 0, False)
        moves = [(g, (g + k) % groups) for g in range(groups)]
        pieces.append(lax.ppermute(piece, "group", moves).astype(F32))
    first = sum(pieces)
    first = lax.optimization_barrier(first)
    received = near_core(lax.all_to_all(out, both, 0, 0, tiled=True))
    lanes = jnp.concatenate(
        [
            lists[:, :8].reshape(-1),
            jnp.pad(lists[:, 8:], ((0, 0), (0, 4)), constant_values=-1).reshape(-1),
        ]
    ).reshape(1, table)
    d_pre, terms = call_owner(received, lanes, far_core(slope), x_self, x_agg, bias)
    grad_self, grad_agg = call_inputs(d_pre, w_self, w_nbr)
    near = jnp.sum(lax.all_to_all(terms, "group", 0, 0, tiled=True).astype(F32), axis=0)
    sums = near[128:144] + near[144:160]
    far = jnp.concatenate(
        [
            first.reshape(4, 32, 3, 128).transpose(1, 0, 2, 3).reshape(32, 12, 128),
            near[0:128].reshape(2, 32, 2, 128).transpose(1, 0, 2, 3).reshape(32, 4, 128),
            jnp.broadcast_to(sums[None], (32, 16, 128)),
        ],
        axis=1,
    ).astype(BF16)
    mine = jnp.sum(lax.all_to_all(far, "inner", 0, 0, tiled=True).astype(F32), axis=0) / pairs
    return (
        grad_self,
        grad_agg,
        mine[0:12].reshape(4, 3, 128).transpose(1, 0, 2).reshape(-1),
        mine[12:16].reshape(2, 2, 128).transpose(1, 0, 2).reshape(-1),
        mine[16:30].reshape(-1),
    )


def solution(mesh):
    both = ("group", "inner")
    return jax.shard_map(
        body,
        mesh=mesh,
        in_specs=(
            P(both, None), P(both, None), P(), P(), P(), P(), P(), P(), P(), P(),
            P(both, None, None), P(both, None), P(both, None),
        ),
        out_specs=(P(both, None), P(both, None), P(both), P(both), P()),
        check_vma=False,
    )
```

```python
import jax
import jax.numpy as jnp
from jax import lax
from jax.experimental import pallas as pl
from jax.experimental.pallas import tpu as pltpu
from jax.sharding import PartitionSpec as P


PAIRS = 2560
UNROLL = 16
STEP = 32
U2 = 4
PARAMS = pltpu.CompilerParams(vmem_limit_bytes=36 * 1024 * 1024)
WIDE = pltpu.CompilerParams(vmem_limit_bytes=60 * 1024 * 1024)
F32 = jnp.float32
BF16 = jnp.bfloat16


def dot(a, b):
    return jnp.dot(a, b, preferred_element_type=F32)


def dot_first(a, b):
    return lax.dot_general(a, b, (((0,), (0,)), ((), ())), preferred_element_type=F32)


def dot_last(a, b):
    return lax.dot_general(a, b, (((1,), (1,)), ((), ())), preferred_element_type=F32)


def sigm(v):
    return 0.5 + 0.5 * jnp.tanh(0.5 * v)


def one_hot(a, b):
    return jnp.where(a == b, 1.0, 0.0).astype(BF16)


def column(block, offset, period):
    count, caps = block.shape
    wide = jnp.broadcast_to(block[:, None, :], (count, 8, caps)).reshape(count * 8, caps)
    want = lax.broadcasted_iota(jnp.int32, wide.shape, 0) % period + offset
    lane = lax.broadcasted_iota(jnp.int32, wide.shape, 1)
    return jnp.sum(jnp.where(lane == want, wide, 0.0), axis=1, keepdims=True)


def layer_kernel(far_xs, far_xa, ws, wn, bl, lists, sent, far_slope, xs, xa, slope, tab, send, sems, loads, saves):
    nodes = xs.shape[0]
    steps = nodes // 256

    def load(r, k):
        rows = pl.ds(r * 256, 256)
        far, near = ((far_xs, xs), (far_xa, xa))[k]
        return pltpu.make_async_copy(far.at[rows], near.at[rows], loads.at[k, r])

    def save(r):
        rows = pl.ds(r * 256, 256)
        return pltpu.make_async_copy(slope.at[rows], far_slope.at[rows], saves.at[r])

    for r in range(steps):
        load(r, 0).start()
        load(r, 1).start()
    for r in range(steps):
        rows = pl.ds(r * 256, 256)
        load(r, 0).wait()
        load(r, 1).wait()
        pre = dot(xs[rows, :], ws[...]) + dot(xa[rows, :], wn[...]) + bl[...]
        s = sigm(pre)
        t = pre * s
        tab[rows, :] = t.astype(BF16)
        slope[rows, :] = s + t * (1.0 - s)
        save(r).start()
    owners = send.shape[0]
    copies = []
    node_ids = lax.broadcasted_iota(jnp.int32, (256, nodes), 1).astype(F32)

    low = lax.broadcasted_iota(jnp.int32, (256, 128), 0) % 8 < 4
    for b in range(owners // 32):
        mine = jnp.transpose(lists[:, b, :].astype(F32))
        at = slice(b * 32, b * 32 + 32)
        y = dot(one_hot(column(mine, 0, 8), node_ids), tab[...]).astype(BF16)
        send[at, 0:8, :] = y[:, :128].reshape(32, 8, 128)
        send[at, 8:16, :] = y[:, 128:].reshape(32, 8, 128)
        y = dot(one_hot(column(mine, 8, 4), node_ids), tab[...])
        y = jnp.where(low, y[:, :128], y[:, 128:]).astype(BF16)
        send[at, 16:24, :] = y.reshape(32, 8, 128)
        copies.append(pltpu.make_async_copy(send.at[pl.ds(b * 32, 32)], sent.at[pl.ds(b * 32, 32)], sems.at[b]))
        copies[-1].start()
    for copy in copies:
        copy.wait()
    for r in range(steps):
        save(r).wait()


def unpack(chunks, rows_ref):
    half = chunks.shape[0] * 8
    rows_ref[0:half, 0:128] = chunks[:, 0:8, :].reshape(half, 128)
    rows_ref[0:half, 128:256] = chunks[:, 8:16, :].reshape(half, 128)
    tail = chunks[:, 16:24, :].reshape(half, 128).astype(F32)
    rows_ref[half:, 0:128] = tail.astype(BF16)
    rows_ref[half:, 128:256] = pltpu.roll(tail, half - 4, 0).astype(BF16)


def pair_blocks(ends, right, joint, h1, sl1, a1, a2, d1, d2, ncol, nlane, w1, b1, w2, b2, wo, grads, gw1, gw2, bias):
    pos = ends.shape[0] // 2
    src = ends.at[0:pos, :]
    dst = ends.at[pos : 2 * pos, :]

    def block(label):
        joint[...] = (src[...].astype(F32) * right[...].astype(F32)).astype(BF16)
        a1[...] = dot(joint[...], w1[...]) + b1[...]

        def first(c, carry):
            at = pl.ds(c * STEP, STEP)
            v = a1[at, :]
            s = sigm(v)
            h = v * s
            h1[at, :] = h.astype(BF16)
            sl1[at, :] = s + h * (1.0 - s)
            return carry

        lax.fori_loop(0, pos // STEP, first, 0, unroll=UNROLL)
        a2[...] = dot(h1[...], w2[...]) + b2[...]
        zero = jnp.zeros((8, w2.shape[1]), F32)

        def fold(d):
            return jnp.sum(d.reshape(STEP // 8, 8, -1), axis=0)

        def second(c, carry):
            at = pl.ds(c * STEP, STEP)
            v = a2[at, :]
            s = sigm(v)
            h = v * s
            score = jnp.sum(h * wo[...], axis=1, keepdims=True)
            ls = sigm(score) - label
            d = ls * wo[...] * (s + h * (1.0 - s))
            d2[at, :] = d.astype(BF16)
            if grads is not None:
                return carry
            return (carry[0] + fold(d), carry[1] + fold(ls * h))

        start = 0 if grads is not None else (zero, zero)
        sums = lax.fori_loop(0, pos // STEP, second, start, unroll=UNROLL)
        a1[...] = dot_last(d2[...], w2[...])

        def third(c, carry):
            at = pl.ds(c * STEP, STEP)
            d = a1[at, :] * sl1[at, :]
            d1[at, :] = d.astype(BF16)
            return carry if grads is not None else carry + fold(d)

        start = 0 if grads is not None else zero
        sum1 = lax.fori_loop(0, pos // STEP, third, start, unroll=UNROLL)
        if grads is None:
            bias[0:8, :] += sum1
            bias[8:16, :] += sums[0]
            bias[16:24, :] += sums[1]
            gw1[...] += dot_first(joint[...], d1[...])
            gw2[...] += dot_first(h1[...], d2[...])
            return None
        dj = dot_last(d1[...], w1[...])
        grads[0:pos, :] += dj * right[...].astype(F32)
        return dj * src[...].astype(F32)

    right[...] = dst[...]
    d_right = block(1.0)
    if grads is not None:
        grads[pos:, :] += d_right
    col_ids = lax.broadcasted_iota(jnp.int32, (pos, pos), 1)
    row_ids = lax.broadcasted_iota(jnp.int32, (pos, pos), 0)

    def negative(k, carry):
        right[...] = dot(one_hot(ncol[pl.ds(k * pos, pos), :], col_ids), dst[...]).astype(BF16)
        d_right = block(0.0)
        if grads is not None:
            grads[pos:, :] += dot(one_hot(nlane[pl.ds(k, 1), :], row_ids), d_right.astype(BF16))
        return carry

    lax.fori_loop(0, ncol.shape[0] // pos, negative, 0)


def slot_blocks(ends, bufs, ncol, nlane, w1, b1, w2, b2, wo, grads):
    pos = ends.shape[0] // 2
    src = ends.at[0:pos, :]
    dst = ends.at[pos : 2 * pos, :]
    chunks = [slice(c * STEP, c * STEP + STEP) for c in range(pos // STEP)]

    def stages(k):
        right, joint, h1, sl1, a1, a2, d1, d2 = bufs[k % 2]
        label = 1.0 if k == 0 else 0.0
        if k == 0:
            right[...] = dst[...]
        else:
            cols = lax.broadcasted_iota(jnp.int32, (pos, pos), 1)
            right[...] = dot(one_hot(ncol[(k - 1) * pos : k * pos, :], cols), dst[...]).astype(BF16)
        joint[...] = (src[...].astype(F32) * right[...].astype(F32)).astype(BF16)
        a1[...] = dot(joint[...], w1[...]) + b1[...]
        yield
        for at in chunks:
            v = a1[at, :]
            s = sigm(v)
            h = v * s
            h1[at, :] = h.astype(BF16)
            sl1[at, :] = s + h * (1.0 - s)
        yield
        a2[...] = dot(h1[...], w2[...]) + b2[...]
        yield
        for at in chunks:
            v = a2[at, :]
            s = sigm(v)
            h = v * s
            score = jnp.sum(h * wo[...], axis=1, keepdims=True)
            ls = sigm(score) - label
            d2[at, :] = (ls * wo[...] * (s + h * (1.0 - s))).astype(BF16)
        yield
        a1[...] = dot_last(d2[...], w2[...])
        yield
        for at in chunks:
            d1[at, :] = (a1[at, :] * sl1[at, :]).astype(BF16)
        yield
        dj = dot_last(d1[...], w1[...])
        grads[0:pos, :] += dj * right[...].astype(F32)
        d_right = dj * src[...].astype(F32)
        if k == 0:
            grads[pos:, :] += d_right
        else:
            rows = lax.broadcasted_iota(jnp.int32, (pos, pos), 0)
            grads[pos:, :] += dot(one_hot(nlane[k - 1 : k, :], rows), d_right.astype(BF16))
        yield

    count = 1 + nlane.shape[0]
    plan = sorted((7 * (k // 2) + k % 2 + t, k % 2 == 0, k) for k in range(count) for t in range(7))
    running = [stages(k) for k in range(count)]
    for _, _, k in plan:
        next(running[k])


def slots_kernel(
    chunks, pcol, plane, ncol, nlane, far_w1, b1, far_w2, b2, wo,
    sent, far_ends,
    rows, grads, split, out, sems, ends, w1, w2, others, *bufs,
):
    owners = chunks.shape[0]
    table = owners * 16
    pos = ends.shape[0] // 2
    load_w1 = pltpu.make_async_copy(far_w1, w1, others.at[0])
    load_w2 = pltpu.make_async_copy(far_w2, w2, others.at[1])
    load_w1.start()
    load_w2.start()
    unpack(chunks, rows)
    slot_ids = lax.broadcasted_iota(jnp.int32, (256, table), 1)

    def fetch(b, carry):
        at = pl.ds(b * 256, 256)
        ends[at, :] = dot(one_hot(pcol[at, :], slot_ids), rows[...]).astype(BF16)
        return carry

    lax.fori_loop(0, 2 * pos // 256, fetch, 0, unroll=U2)
    save_ends = pltpu.make_async_copy(ends, far_ends, others.at[2])
    save_ends.start()
    load_w1.wait()
    load_w2.wait()
    grads[...] = jnp.zeros_like(grads)
    slot_blocks(ends, (bufs[:8], bufs[8:]), ncol, nlane, w1, b1, w2, b2, wo, grads)
    split[...] = grads[...].astype(BF16)
    sub = lax.broadcasted_iota(jnp.int32, (256, 2 * pos), 0)
    sub_mixed = sub - (sub & 4)

    def spread(ids):
        return dot(one_hot(plane[...], ids), split[...])

    low = lax.broadcasted_iota(jnp.int32, (256, 128), 0) % 8 < 4
    copies = []
    for b in range(owners // 32):
        at = slice(b * 32, b * 32 + 32)
        y = spread(sub + b * 256).astype(BF16)
        out[at, 0:8, :] = y[:, :128].reshape(32, 8, 128)
        out[at, 8:16, :] = y[:, 128:].reshape(32, 8, 128)
        y = spread(sub_mixed + (owners * 8 + b * 256))
        y = jnp.where(low, y[:, :128], y[:, 128:]).astype(BF16)
        out[at, 16:24, :] = y.reshape(32, 8, 128)
        copies.append(pltpu.make_async_copy(out.at[pl.ds(b * 32, 32)], sent.at[pl.ds(b * 32, 32)], sems.at[b]))
        copies[-1].start()
    for copy in copies:
        copy.wait()
    save_ends.wait()


def weights_kernel(
    ends, ncol, w1, b1, w2, b2, wo,
    scorer, bias,
    right, joint, h1, sl1, a1, a2, d1, d2, gw1, gw2,
):
    gw1[...] = jnp.zeros_like(gw1)
    gw2[...] = jnp.zeros_like(gw2)
    bias[...] = jnp.zeros_like(bias)
    pair_blocks(
        ends, right, joint, h1, sl1, a1, a2, d1, d2, ncol, None, w1, b1, w2, b2, wo, None, gw1, gw2, bias
    )
    for g in range(8):
        for q in range(4):
            cols = slice(q * 128, q * 128 + 128)
            lo_row = g * 96
            at = q * 96
            n1 = min(max(256 - lo_row, 0), 96)
            if n1 > 0:
                scorer[g, at : at + n1, :] = gw1[lo_row : lo_row + n1, cols].astype(BF16)
            if n1 < 96:
                first_row = lo_row + n1 - 256
                scorer[g, at + n1 : at + 96, :] = gw2[first_row : first_row + 96 - n1, cols].astype(BF16)


def owner_kernel(
    chunks, lanes, far_slope, xs, xa, bias,
    dpre, terms,
    rows, sums, slope, sem,
):
    table = lanes.shape[1]
    nodes = xs.shape[0]
    load = pltpu.make_async_copy(far_slope, slope, sem.at[0])
    load.start()
    unpack(chunks, rows)
    load.wait()
    ids = lax.broadcasted_iota(jnp.int32, (256, table), 0)

    def nodes_step(b, carry):
        at = pl.ds(b * 256, 256)
        d = dot(one_hot(lanes[...], ids + b * 256), rows[...]) * slope[at, :]
        low = d.astype(BF16)
        dpre[at, :] = low
        return carry + jnp.sum(d.reshape(32, 8, 256), axis=0)

    total = lax.fori_loop(0, nodes // 256, nodes_step, jnp.zeros((8, 256), F32))
    total = jnp.sum(total, axis=0, keepdims=True)
    sums[...] = jnp.zeros_like(sums)
    for part in range(3):
        whole = jnp.sum(bias[part * 8 : part * 8 + 8, :], axis=0, keepdims=True)
        for q in range(4):
            sums[part * 4 + q : part * 4 + q + 1, :] = whole[:, q * 128 : q * 128 + 128]
    for q in range(2):
        sums[12 + q : 13 + q, :] = total[:, q * 128 : q * 128 + 128]
    hi = sums[0:16, :].astype(BF16)
    lo = (sums[0:16, :] - hi.astype(F32)).astype(BF16)
    parts = (dot_first(xs[...], dpre[...]), dot_first(xa[...], dpre[...]))
    for g in range(8):
        mine = parts[g // 4]
        r = (g % 4) * 64
        for q in range(2):
            terms[g, q * 64 : q * 64 + 64, :] = mine[r : r + 64, q * 128 : q * 128 + 128].astype(BF16)
        terms[g, 128:144, :] = hi
        terms[g, 144:160, :] = lo


def inputs_kernel(dpre, ws, wn, gself, gagg):
    gself[...] = dot_last(dpre[...], ws[...]).astype(BF16)
    gagg[...] = dot_last(dpre[...], wn[...]).astype(BF16)


def final_kernel(parts, scorer, layer, bias):
    total = jnp.sum(parts[...].astype(F32), axis=0) / PAIRS
    for r in range(3):
        for q in range(4):
            at = (r * 4 + q) * 128
            scorer[at : at + 128] = total[q * 3 + r, :]
    for r in range(2):
        for q in range(2):
            at = (r * 2 + q) * 128
            layer[at : at + 128] = total[12 + q * 2 + r, :]
    for k in range(14):
        bias[k * 128 : k * 128 + 128] = total[16 + k, :]


def call_final(parts):
    return pl.pallas_call(
        final_kernel,
        out_shape=(
            jax.ShapeDtypeStruct((1536,), F32),
            jax.ShapeDtypeStruct((512,), F32),
            jax.ShapeDtypeStruct((1792,), F32),
        ),
        compiler_params=PARAMS,
        name="final",
    )(parts)


def call_layer(*args):
    nodes, width = args[0].shape
    owners = args[5].shape[1] * args[5].shape[2]
    return pl.pallas_call(
        layer_kernel,
        out_shape=(
            pltpu.HBM((owners, 24, 128), BF16),
            pltpu.HBM((nodes, width), F32),
        ),
        in_specs=[pl.BlockSpec(memory_space=pltpu.HBM)] * 2 + [pl.BlockSpec(memory_space=pltpu.VMEM)] * 4,
        out_specs=(pl.BlockSpec(memory_space=pltpu.HBM), pl.BlockSpec(memory_space=pltpu.HBM)),
        scratch_shapes=[
            pltpu.VMEM((nodes, width), BF16),
            pltpu.VMEM((nodes, width), BF16),
            pltpu.VMEM((nodes, width), F32),
            pltpu.VMEM((nodes, width), BF16),
            pltpu.VMEM((owners, 24, 128), BF16),
            pltpu.SemaphoreType.DMA((owners // 32,)),
            pltpu.SemaphoreType.DMA((2, nodes // 256)),
            pltpu.SemaphoreType.DMA((nodes // 256,)),
        ],
        compiler_params=WIDE,
        name="layer",
    )(*args)


def block_scratch(pos, width, hidden):
    return [
        pltpu.VMEM((pos, width), BF16),
        pltpu.VMEM((pos, width), BF16),
        pltpu.VMEM((pos, hidden), BF16),
        pltpu.VMEM((pos, hidden), F32),
        pltpu.VMEM((pos, hidden), F32),
        pltpu.VMEM((pos, hidden), F32),
        pltpu.VMEM((pos, hidden), BF16),
        pltpu.VMEM((pos, hidden), BF16),
    ]


def call_slots(*args):
    owners = args[0].shape[0]
    pos = args[2].shape[1] // 2
    width, hidden = args[5].shape
    return pl.pallas_call(
        slots_kernel,
        out_shape=(
            pltpu.HBM((owners, 24, 128), BF16),
            pltpu.HBM((2 * pos, width), BF16),
        ),
        in_specs=[pl.BlockSpec(memory_space=pltpu.HBM if k in (5, 7) else pltpu.VMEM) for k in range(10)],
        out_specs=(pl.BlockSpec(memory_space=pltpu.HBM), pl.BlockSpec(memory_space=pltpu.HBM)),
        scratch_shapes=[
            pltpu.VMEM((owners * 16, width), BF16),
            pltpu.VMEM((2 * pos, width), F32),
            pltpu.VMEM((2 * pos, width), BF16),
            pltpu.VMEM((owners, 24, 128), BF16),
            pltpu.SemaphoreType.DMA((owners // 32,)),
            pltpu.VMEM((2 * pos, width), BF16),
            pltpu.VMEM((width, hidden), BF16),
            pltpu.VMEM((hidden, hidden), BF16),
            pltpu.SemaphoreType.DMA((3,)),
        ]
        + block_scratch(pos, width, hidden) * 2,
        compiler_params=PARAMS,
        name="slots",
    )(*args)


def call_weights(*args):
    pos = args[0].shape[0] // 2
    width, hidden = args[2].shape
    return pl.pallas_call(
        weights_kernel,
        out_shape=(
            jax.ShapeDtypeStruct((8, 384, 128), BF16),
            jax.ShapeDtypeStruct((24, hidden), F32),
        ),
        scratch_shapes=block_scratch(pos, width, hidden)
        + [pltpu.VMEM((width, hidden), F32), pltpu.VMEM((hidden, hidden), F32)],
        compiler_params=PARAMS,
        name="weights",
    )(*args)


def call_owner(*args):
    nodes, width = args[3].shape
    table = args[1].shape[1]
    return pl.pallas_call(
        owner_kernel,
        out_shape=(
            jax.ShapeDtypeStruct((nodes, width), BF16),
            pltpu.HBM((8, 160, 128), BF16),
        ),
        in_specs=[pl.BlockSpec(memory_space=pltpu.HBM if k == 2 else pltpu.VMEM) for k in range(6)],
        scratch_shapes=[
            pltpu.VMEM((table, width), BF16),
            pltpu.VMEM((16, 128), F32),
            pltpu.VMEM((nodes, width), F32),
            pltpu.SemaphoreType.DMA((1,)),
        ],
        compiler_params=PARAMS,
        name="owner",
    )(*args)


def call_inputs(*args):
    return pl.pallas_call(
        inputs_kernel,
        out_shape=(
            jax.ShapeDtypeStruct(args[0].shape, BF16),
            jax.ShapeDtypeStruct(args[0].shape, BF16),
        ),
        compiler_params=PARAMS,
        name="inputs",
    )(*args)


def far_core(x):
    return pltpu.with_memory_space_constraint(x, pltpu.HBM)


def near_core(x):
    return pltpu.with_memory_space_constraint(x, pltpu.VMEM)


def body(
    x_self, x_agg, w_self, w_nbr, b_layer, w_one, b_one, w_two, b_two, w_out,
    send_lists, endpoint_slots, neg_index,
):
    both = ("group", "inner")
    owners = lax.axis_size("group") * lax.axis_size("inner")
    pos = endpoint_slots.shape[0]
    negs = neg_index.shape[1]
    assert pos * (1 + negs) == PAIRS
    table = owners * 16
    lists = send_lists.reshape(owners, 12)
    groups = lax.axis_size("group")
    out_vector = lax.ppermute(w_out, "group", [(g, (g + 1) % groups) for g in range(groups)])
    send, slope = call_layer(far_core(x_self), far_core(x_agg), w_self, w_nbr, b_layer.reshape(1, -1), send_lists.transpose(2, 0, 1))
    w_one_far, w_two_far = far_core(w_one), far_core(w_two)
    fetched = near_core(lax.all_to_all(send, both, 0, 0, tiled=True))
    owner = endpoint_slots // 12
    column = endpoint_slots - owner * 12
    place = jnp.where(column < 8, owner * 8 + column, owners * 8 + owner * 8 + column - 8)
    place = place.T.reshape(-1)
    neg_t = neg_index.T
    ncol = neg_t.reshape(-1, 1)
    scorer_args = (w_one, b_one.reshape(1, -1), w_two, b_two.reshape(1, -1), out_vector.reshape(1, -1))
    out, ends = call_slots(fetched, place.reshape(-1, 1), place.reshape(1, -1), ncol, neg_t, w_one_far, scorer_args[1], w_two_far, *scorer_args[3:])
    scorer, bias = call_weights(ends, ncol, *scorer_args)
    here = lax.axis_index("group")
    pieces = [lax.dynamic_index_in_dim(scorer, here, 0, False).astype(F32)]
    for k in range(1, groups):
        piece = lax.dynamic_index_in_dim(scorer, (here + k) % groups, 0, False)
        moves = [(g, (g + k) % groups) for g in range(groups)]
        pieces.append(lax.ppermute(piece, "group", moves).astype(F32))
    first = sum(pieces)
    first = lax.optimization_barrier(first)
    received = near_core(lax.all_to_all(out, both, 0, 0, tiled=True))
    lanes = jnp.concatenate(
        [
            lists[:, :8].reshape(-1),
            jnp.pad(lists[:, 8:], ((0, 0), (0, 4)), constant_values=-1).reshape(-1),
        ]
    ).reshape(1, table)
    d_pre, terms = call_owner(received, lanes, far_core(slope), x_self, x_agg, bias)
    grad_self, grad_agg = call_inputs(d_pre, w_self, w_nbr)
    near = jnp.sum(lax.all_to_all(terms, "group", 0, 0, tiled=True).astype(F32), axis=0)
    sums = near[128:144] + near[144:160]
    far = jnp.concatenate(
        [
            first.reshape(4, 32, 3, 128).transpose(1, 0, 2, 3).reshape(32, 12, 128),
            near[0:128].reshape(2, 32, 2, 128).transpose(1, 0, 2, 3).reshape(32, 4, 128),
            jnp.broadcast_to(sums[None], (32, 16, 128)),
        ],
        axis=1,
    ).astype(BF16)
    scorer_share, layer_share, bias_total = call_final(lax.all_to_all(far, "inner", 0, 0, tiled=True))
    return grad_self, grad_agg, scorer_share, layer_share, bias_total


def solution(mesh):
    both = ("group", "inner")
    return jax.shard_map(
        body,
        mesh=mesh,
        in_specs=(
            P(both, None), P(both, None), P(), P(), P(), P(), P(), P(), P(), P(),
            P(both, None, None), P(both, None), P(both, None),
        ),
        out_specs=(P(both, None), P(both, None), P(both), P(both), P()),
        check_vma=False,
    )
```
